256 devices in a mesh: dp: 16 (over z_lo, x), seq: 16 (over z_hi, y, core).
Axes of the slice: x: 4, y: 4, z: 8 (z_hi: 2, z_lo: 4; z = z_hi * 4 + z_lo), core: 2. Of those that a mesh axis runs over, the one named last changes fastest.
Arguments:
- queries: bfloat16 [16, 2048, 2048], P('dp', 'seq'), may hold values from -5 to 5
- key_states: bfloat16 [16, 2048, 2048], P('dp', 'seq'), may hold values from -5 to 5
- value_states: bfloat16 [16, 2048, 2048], P('dp', 'seq'), may hold values from -6 to 6
- residual: bfloat16 [16, 2048, 2048], P('dp', 'seq'), may hold values from -6 to 6
- enc_hidden: bfloat16 [16, 2048, 1536], P('dp', 'seq'), may hold values from -6 to 6
- enc_gain: float32 [1536], replicated, may hold values from 0.1 to 1.9
- enc_bias: float32 [1536], replicated, may hold values from -0.5 to 0.5
- feature_target: int32 [16, 2048], P('dp', 'seq'), may hold values from 0 to 2047, as said below
- timestep: int32 [16], P('dp'), may hold values from 0 to 999
- gate_weight: bfloat16 [256, 2048], P('dp'), may hold values from -0.375 to 0.375
- lift_weight: bfloat16 [2048, 1024], P('dp'), may hold values from -0.125 to 0.125
- out_weight: bfloat16 [1024, 1536], P('dp'), may hold values from -0.1875 to 0.1875
Outputs:
- d_queries: bfloat16 [16, 2048, 2048], P('dp', 'seq')
- d_keys: bfloat16 [16, 2048, 2048], P('dp', 'seq')
- d_values: bfloat16 [16, 2048, 2048], P('dp', 'seq')
- grad_gate: float32 [256, 2048], P('dp')
- grad_lift: float32 [2048, 1024], P('dp')
- grad_out: float32 [1024, 1536], P('dp')
The draws below stay inside these ranges and needn't reach their ends.
Inputs may be any that keep to these rules, and one draw needn't show every extreme that they name: For each clip, feature_target is a permutation of its 2048 token positions. The 128 encoder rows of one device of seq target at most 16 tokens held by any one device of seq, and exactly 16 for some.
All inputs are finite; a program needn't handle non-finite values.
Results may differ from the reference program's by a relative error of at most 0.02.
Values may be sent and summed in bfloat16 or wider, within the bound.
A program may use at most 128 MiB of HBM per device.

```python
import math
import jax
import jax.numpy as jnp
from jax import lax

TOK_DEV = 128
HEADS = 16
HD = 128
PH = 1024
ZD = 1536
TEMB = 256
CLIPS = 16
LEN = 2048
FEAT = 2048


def pattern_draw(key, which):
    own = jax.random.fold_in(key, which)
    values = jnp.clip(jax.random.normal(own, (CLIPS, LEN, FEAT), jnp.float32), -5.0, 5.0)
    return values.astype(jnp.bfloat16)


def draw_queries(key, part):
    return pattern_draw(key, 1)


def draw_key_states(key, part):
    return pattern_draw(key, 2)


def draw_feature_target(key, part):
    groups = LEN // TOK_DEV
    share = TOK_DEV // groups

    def one_clip(clip_key):
        first = jax.random.fold_in(clip_key, 1)
        second = jax.random.fold_in(clip_key, 2)
        third = jax.random.fold_in(clip_key, 3)
        fourth = jax.random.fold_in(clip_key, 4)
        primary = jax.random.permutation(first, groups)
        offset = jax.random.randint(second, (), 1, groups)
        lesser = (primary + offset) % groups
        devices = jnp.arange(groups)
        counts = share + share * (devices[None, :] == primary[:, None]).astype(jnp.int32) - share * (devices[None, :] == lesser[:, None]).astype(jnp.int32)
        bounds = jnp.cumsum(counts, axis=1)
        slots = jnp.arange(TOK_DEV)
        owning = jnp.sum((bounds[:, None, :] <= slots[None, :, None]).astype(jnp.int32), axis=2)
        shuffle = jax.vmap(lambda sub_key: jax.random.permutation(sub_key, TOK_DEV))(jax.random.split(third, groups))
        owning = jnp.take_along_axis(owning, shuffle, axis=1).reshape(LEN)
        positions = jnp.arange(LEN)
        ranked = jnp.argsort(owning * LEN + positions, stable=True)
        within = jax.vmap(lambda sub_key: jax.random.permutation(sub_key, TOK_DEV))(jax.random.split(fourth, groups)).reshape(LEN)
        placed = positions // TOK_DEV * TOK_DEV + within
        return jnp.zeros((LEN,), jnp.int32).at[ranked].set(placed.astype(jnp.int32))
    return jax.vmap(one_clip)(jax.random.split(key, CLIPS))


def set_ends(entries, key, low, largest):
    dims = entries.shape
    spot = [jax.random.randint(jax.random.fold_in(key, axis), (), 0, dims[axis]) for axis in range(len(dims))]
    entries = entries.at[tuple(spot)].set(low)
    longest = dims.index(max(dims))
    spot[longest] = (spot[longest] + 1) % dims[longest]
    return entries.at[tuple(spot)].set(largest)


def strengthened(result, key, source, target, blocks, factor):
    def block_of(dim):
        return (jnp.arange(result.shape[dim]) // (result.shape[dim] // blocks)).reshape((-1,) + (1,) * (result.ndim - 1 - dim))

    one_side = jax.random.permutation(key, blocks)[block_of(target)]
    second = (block_of(target) + blocks // 2) % blocks
    return jnp.where((block_of(source) == one_side) | (block_of(source) == second), factor * result, result)


def level_of(rng, dims, cuts, least, largest):
    level, own = 1.0, jax.random.fold_in(rng, 6)
    for dim, blocks in cuts:
        heights = jnp.exp(jax.random.uniform(jax.random.fold_in(own, dim), (blocks,), jnp.float32, least / len(cuts), largest / len(cuts)))
        level = level * jnp.repeat(heights, dims[dim] // blocks).reshape([-1 if axis == dim else 1 for axis in range(len(dims))])
    return level


def noise(own_key, dims, deviation, limit, cuts=(), kind=jnp.bfloat16):
    values = deviation * jax.random.normal(own_key, dims, jnp.float32)
    if cuts:
        values = values * level_of(own_key, dims, cuts, -0.22, 0.18)
    return jnp.clip(values, -limit, limit).astype(kind)


def noise_with(rng, extent, scale, most, cuts, heavy, dtype=jnp.bfloat16):
    drawn = scale * jax.random.normal(rng, extent, jnp.float32)
    if cuts:
        drawn = drawn * level_of(rng, extent, cuts, -0.22, 0.18)
    return jnp.clip(strengthened(drawn, jax.random.fold_in(rng, 3), *heavy), -most, most).astype(dtype)


def setup_inputs(seed: int = 0) -> dict:
    key_of = jax.random.split(jax.random.key(seed), 13)
    queries = draw_queries(jax.random.fold_in(key_of[12], 71), 0)
    key_states = draw_key_states(jax.random.fold_in(key_of[12], 71), 0)
    value_states = noise(key_of[2], (CLIPS, LEN, FEAT), 1.0, 6.0, ((0, 16), (1, 16)))
    residual = noise_with(key_of[3], (CLIPS, LEN, FEAT), 1.0, 6.0, ((0, 16), (1, 16)), (0, 2, 16, 2.0))
    enc_hidden = noise(key_of[4], (CLIPS, LEN, ZD), 1.0, 6.0, ((0, 16), (1, 16)))
    enc_gain = jnp.clip(1.0 + 0.18 * jax.random.normal(key_of[5], (ZD,), jnp.float32), 0.1, 1.9)
    enc_bias = jnp.clip(jax.random.uniform(key_of[6], (ZD,), jnp.float32, -0.5, 0.5), -0.5, 0.5)
    feature_target = draw_feature_target(jax.random.fold_in(key_of[12], 71), 0)
    timestep = set_ends(jax.random.randint(key_of[8], (CLIPS,), 0, 1000), jax.random.fold_in(key_of[8], 1), 0, 999).astype(jnp.int32)
    gate_weight = noise(key_of[9], (TEMB, FEAT), TEMB ** -0.5, 0.375, ((0, 16),))
    lift_weight = noise(key_of[10], (FEAT, PH), FEAT ** -0.5, 0.125, ((0, 16),))
    out_weight = noise(key_of[11], (PH, ZD), PH ** -0.5, 0.1875, ((0, 16),))
    return {"queries": queries, "key_states": key_states, "value_states": value_states, "residual": residual, "enc_hidden": enc_hidden, "enc_gain": enc_gain, "enc_bias": enc_bias, "feature_target": feature_target, "timestep": timestep, "gate_weight": gate_weight, "lift_weight": lift_weight, "out_weight": out_weight}


EPSILON = 1e-06

def rounded(array):
    return lax.optimization_barrier(array.astype(jnp.bfloat16)).astype(jnp.float32)

def embed_time(timestep):
    half_width = TEMB // 2
    frequency = jnp.exp(-math.log(10000.0) * jnp.arange(half_width).astype(jnp.float32) / half_width)
    angles = timestep.astype(jnp.float32)[:, None] * frequency[None, :]
    return jnp.concatenate([jnp.cos(angles), jnp.sin(angles)], axis=1).astype(jnp.bfloat16)

def encoder_norm(hidden, enc_gain, enc_bias):
    widened = hidden.astype(jnp.float32)
    centred = widened - lax.optimization_barrier(jnp.mean(widened, axis=-1, keepdims=True))
    variance = lax.optimization_barrier(jnp.mean(centred * centred, axis=-1, keepdims=True))
    return (centred * lax.rsqrt(variance + EPSILON) * enc_gain + enc_bias).astype(jnp.bfloat16)

def soft_scores(query_block, key_heads):
    scores = jnp.einsum('bhd,lhd->hbl', query_block.astype(jnp.float32), key_heads.astype(jnp.float32)) * HD ** (-0.5)
    shifted = jnp.exp(scores - lax.optimization_barrier(jnp.max(scores, axis=-1, keepdims=True)))
    return shifted / lax.optimization_barrier(jnp.sum(shifted, axis=-1, keepdims=True))

def split_blocks(array):
    length = array.shape[0]
    block_rows = min(length, 512)
    return array.reshape(length // block_rows, block_rows, array.shape[1], array.shape[2])

def attention_forward(query_heads, key_heads, value_heads):

    def one_block(query_block):
        chances = rounded(soft_scores(query_block, key_heads))
        return jnp.einsum('hbl,lhd->bhd', chances, value_heads.astype(jnp.float32)).astype(jnp.bfloat16)
    mixed = lax.map(one_block, split_blocks(query_heads))
    return mixed.reshape(query_heads.shape[0], -1)

def attention_backward(query_heads, key_heads, value_heads, grad_heads):
    key_wide = key_heads.astype(jnp.float32)
    value_wide = value_heads.astype(jnp.float32)

    def one_block(carried, pieces):
        grad_keys, grad_values = carried
        query_block, grad_block = pieces
        chances = soft_scores(query_block, key_heads)
        grad_wide = grad_block.astype(jnp.float32)
        grad_chances = jnp.einsum('bhd,lhd->hbl', grad_wide, value_wide)
        grad_values = grad_values + jnp.einsum('hbl,bhd->lhd', rounded(chances), grad_wide)
        inner_sum = lax.optimization_barrier(jnp.sum(grad_chances * chances, axis=-1, keepdims=True))
        grad_scores = rounded(chances * (grad_chances - inner_sum) * HD ** (-0.5))
        grad_query = jnp.einsum('hbl,lhd->bhd', grad_scores, key_wide)
        grad_keys = grad_keys + jnp.einsum('hbl,bhd->lhd', grad_scores, query_block.astype(jnp.float32))
        return ((grad_keys, grad_values), grad_query.astype(jnp.bfloat16))
    zeros = jnp.zeros(key_heads.shape, jnp.float32)
    carried, grad_queries = lax.scan(one_block, (zeros, zeros), (split_blocks(query_heads), split_blocks(grad_heads)))
    length = query_heads.shape[0]
    return (grad_queries.reshape(length, -1), carried[0].reshape(length, -1).astype(jnp.bfloat16), carried[1].reshape(length, -1).astype(jnp.bfloat16))

def heads_of(array):
    return array.reshape(array.shape[0], HEADS, HD)

def reference(queries, key_states, value_states, residual, enc_hidden, enc_gain, enc_bias, feature_target, timestep, gate_weight, lift_weight, out_weight):
    embedded = embed_time(timestep)
    gating = jnp.dot(embedded, gate_weight, preferred_element_type=jnp.float32)
    normed = encoder_norm(enc_hidden, enc_gain, enc_bias)

    def place(feature_rows, target_rows):
        return jnp.zeros_like(feature_rows).at[target_rows].set(feature_rows)
    aligned = jax.vmap(place)(normed, feature_target)

    def clip_forward(triple):
        return attention_forward(heads_of(triple[0]), heads_of(triple[1]), heads_of(triple[2]))
    mixed = lax.map(clip_forward, (queries, key_states, value_states))
    hidden = (residual.astype(jnp.float32) + gating[:, None, :] * mixed.astype(jnp.float32)).astype(jnp.bfloat16)
    flat_hidden = hidden.reshape(-1, HEADS * HD)
    lifted = jnp.dot(flat_hidden, lift_weight, preferred_element_type=jnp.float32)
    sigmoid_lift = jax.nn.sigmoid(lifted)
    activated = (lifted * sigmoid_lift).astype(jnp.bfloat16)
    predicted = jnp.dot(activated, out_weight, preferred_element_type=jnp.float32)
    target_wide = aligned.reshape(-1, ZD).astype(jnp.float32)
    pred_norm = jnp.sqrt(lax.optimization_barrier(jnp.sum(predicted * predicted, axis=1, keepdims=True)) + EPSILON)
    target_norm = jnp.sqrt(lax.optimization_barrier(jnp.sum(target_wide * target_wide, axis=1, keepdims=True)) + EPSILON)
    cosine = lax.optimization_barrier(jnp.sum(predicted * target_wide, axis=1, keepdims=True)) / (pred_norm * target_norm)
    grad_pred = (-1.0 * ZD * (target_wide / (pred_norm * target_norm) - cosine * predicted / (pred_norm * pred_norm))).astype(jnp.bfloat16)
    grad_out = jnp.dot(activated.T, grad_pred, preferred_element_type=jnp.float32)
    grad_act = jnp.dot(grad_pred, out_weight.T, preferred_element_type=jnp.float32)
    grad_lifted = (grad_act * sigmoid_lift * (1.0 + lifted * (1.0 - sigmoid_lift))).astype(jnp.bfloat16)
    grad_lift = jnp.dot(flat_hidden.T, grad_lifted, preferred_element_type=jnp.float32)
    grad_hidden = jnp.dot(grad_lifted, lift_weight.T, preferred_element_type=jnp.float32).reshape(CLIPS, LEN, HEADS * HD)
    grad_mixed = (gating[:, None, :] * grad_hidden).astype(jnp.bfloat16)
    grad_gating = lax.optimization_barrier(jnp.sum(grad_hidden * mixed.astype(jnp.float32), axis=1))
    grad_gate = jnp.dot(embedded.astype(jnp.float32).T, grad_gating, precision=lax.Precision.HIGHEST)

    def clip_backward(quad):
        return attention_backward(heads_of(quad[0]), heads_of(quad[1]), heads_of(quad[2]), heads_of(quad[3]))
    back = lax.map(clip_backward, (queries, key_states, value_states, grad_mixed))
    return (back[0], back[1], back[2], grad_gate, grad_lift, grad_out)
```

```python
import functools
import math

import jax
import jax.numpy as jnp
from jax import lax
from jax.experimental import pallas as pl
from jax.experimental.pallas import tpu as pltpu
from jax.sharding import PartitionSpec as P

HD = 128
ZD = 1536
PH = 1024
FEAT = 2048
TEMB = 256
LEN = 2048
TOK = 128
EPSILON = 1e-06
SCALE = HD ** (-0.5)
LOG2 = SCALE * math.log2(math.e)
QB = 256
KB = 256
MESH = pl.DeviceIdType.MESH
F32 = jnp.float32
BF16 = jnp.bfloat16

SCRATCH = dict(
    qh=pltpu.VMEM((LEN, HD), BF16),
    kh=pltpu.VMEM((LEN, HD), BF16),
    vh=pltpu.VMEM((LEN, HD), BF16),
    gcols=pltpu.VMEM((TEMB, HD), BF16),
    embs=pltpu.VMEM((16, 8, TEMB), F32),
    rows_send=pltpu.VMEM((256, ZD + 128), BF16),
    rows_got=pltpu.VMEM((256, ZD + 128), BF16),
    liftf=pltpu.VMEM((4, 4, 128, PH), BF16),
    outf=pltpu.VMEM((4, 4, 64, ZD), BF16),
    o32=pltpu.VMEM((LEN, HD), F32),
    lse=pltpu.VMEM((8, LEN), F32),
    gated=pltpu.VMEM((LEN, HD), BF16),
    mix_tok=pltpu.VMEM((TOK, FEAT), BF16),
    hid2=pltpu.VMEM((2 * TOK, FEAT), BF16),
    act2=pltpu.VMEM((2 * TOK, PH), BF16),
    gpf=pltpu.VMEM((2, TOK, ZD // 2), BF16),
    gp2=pltpu.VMEM((2 * TOK, ZD // 2), BF16),
    glf=pltpu.VMEM((2, TOK, PH // 2), BF16),
    gl2=pltpu.VMEM((2 * TOK, PH // 2), BF16),
    ghs=pltpu.VMEM((TOK, FEAT), BF16),
    gh=pltpu.VMEM((LEN, HD), BF16),
    do=pltpu.VMEM((LEN, HD), BF16),
    drow=pltpu.VMEM((8, LEN), F32),
    dq32=pltpu.VMEM((LEN, HD), F32),
    dqb=pltpu.VMEM((LEN, HD), BF16),
    dkb=pltpu.VMEM((LEN, HD), BF16),
    dvb=pltpu.VMEM((LEN, HD), BF16),
    ggs=pltpu.VMEM((8, HD), F32),
    ggall=pltpu.VMEM((16, 8, HD), F32),
    gfull=pltpu.VMEM((TEMB, HD), F32),
    gsl=pltpu.VMEM((16, HD), F32),
    gl_x=pltpu.VMEM((4, 4, 128, PH // 2), BF16),
    go_x=pltpu.VMEM((4, 4, 64, ZD // 2), BF16),
    rl_x=pltpu.VMEM((3, 4, 128, PH // 2), BF16),
    ro_x=pltpu.VMEM((3, 4, 64, ZD // 2), BF16),
    gl_y=pltpu.VMEM((4, 128, PH // 2), BF16),
    go_y=pltpu.VMEM((4, 64, ZD // 2), BF16),
    rl_y=pltpu.VMEM((3, 4, 32, PH // 2), BF16),
    ro_y=pltpu.VMEM((3, 4, 16, ZD // 2), BF16),
    gl_z=pltpu.VMEM((4, 32, PH // 2), BF16),
    go_z=pltpu.VMEM((4, 16, ZD // 2), BF16),
    rl_z=pltpu.VMEM((7, 32, PH // 2), BF16),
    ro_z=pltpu.VMEM((7, 16, ZD // 2), BF16),
    pl_f=pltpu.VMEM((32, PH // 2), F32),
    po_f=pltpu.VMEM((16, ZD // 2), F32),
    s_a2a=pltpu.SemaphoreType.DMA((8, 16)),
    r_a2a=pltpu.SemaphoreType.DMA((8, 16)),
    s_rel=pltpu.SemaphoreType.DMA((16,)),
    r_rel=pltpu.SemaphoreType.DMA((16,)),
    s_gate=pltpu.SemaphoreType.DMA((4, 16)),
    r_gate=pltpu.SemaphoreType.DMA((4, 16)),
    s_w=pltpu.SemaphoreType.DMA((2, 13)),
    r_w=pltpu.SemaphoreType.DMA((2, 13)),
    s_pair=pltpu.SemaphoreType.DMA((4,)),
    r_pair=pltpu.SemaphoreType.DMA((4,)),
    s_red=pltpu.SemaphoreType.DMA((2, 20)),
    r_red=pltpu.SemaphoreType.DMA((2, 20)),
    local=pltpu.SemaphoreType.DMA((20,)),
)
NAMES = list(SCRATCH)


def dot(a, b, dims, precision=None):
    return lax.dot_general(
        a, b, (dims, ((), ())), precision=precision, preferred_element_type=F32
    )


def step_kernel(*refs):
    q, k, v, res, enc, gain, bias, trow, tcol, emb, gate, lift, outw = refs[:13]
    dq, dk, dv, ggate, glift, gout = refs[13:19]
    s = dict(zip(NAMES, refs[19:]))
    dp, me = lax.axis_index("dp"), lax.axis_index("seq")
    zl, x = lax.div(dp, 4), lax.rem(dp, 4)
    zh, yc = lax.div(me, 8), lax.rem(me, 8)
    y, c = lax.div(yc, 2), lax.rem(yc, 2)
    z = zh * 4 + zl
    partner = (dp, me + 1 - 2 * c)

    def at_x(i):
        return (zl * 4 + lax.rem(x + i, 4), me)

    def at_y(i):
        return (dp, zh * 8 + lax.rem(y + i, 4) * 2 + c)

    def at_z(i):
        to = lax.rem(z + i, 8)
        return (lax.rem(to, 4) * 4 + x, lax.div(to, 4) * 8 + yc)

    def at_yc(i):
        return (dp, zh * 8 + lax.rem(yc + i, 8))

    def cols(j):
        return pl.ds(pl.multiple_of(j * 128, 128), 128)

    def remote(src, dst, send, recv, device):
        return pltpu.make_async_remote_copy(
            src_ref=src, dst_ref=dst, send_sem=send, recv_sem=recv,
            device_id=device, device_id_type=MESH,
        )

    finish = []

    def go(*copy):
        made = remote(*copy)
        made.start()
        finish.append(made.wait_send)
        return made

    barrier = pltpu.get_barrier_semaphore()

    def greet(i, _):
        pl.semaphore_signal(barrier, 1, device_id=(dp, lax.rem(me + i, 16)), device_id_type=MESH)
        pl.semaphore_signal(barrier, 1, device_id=(lax.rem(dp + i, 16), me), device_id_type=MESH)
        return 0

    lax.fori_loop(1, 16, greet, 0)
    for i in range(1, 4):
        other = (lax.rem(zl + i, 4) * 4 + x, (1 - zh) * 8 + yc)
        pl.semaphore_signal(barrier, 1, device_id=other, device_id_type=MESH)
    pl.semaphore_wait(barrier, 33)

    def tok_to_head(t, src, dst):
        def copy(j, owner):
            return remote(
                src.at[:, cols(j)], dst.at[cols(owner), :],
                s["s_a2a"].at[t, j], s["r_a2a"].at[t, owner], (dp, j),
            )

        def start(i, _):
            copy(lax.rem(me + i, 16), me).start()
            return 0

        own = pltpu.make_async_copy(src.at[:, cols(me)], dst.at[cols(me), :], s["local"].at[t])
        own.start()
        lax.fori_loop(1, 16, start, 0)

        def wait():
            def one(i, _):
                j = lax.rem(me + i, 16)
                copy(j, j).wait_recv()
                return 0

            own.wait()
            lax.fori_loop(1, 16, one, 0)

        def sent():
            def one(i, _):
                copy(lax.rem(me + i, 16), me).wait_send()
                return 0

            lax.fori_loop(1, 16, one, 0)

        finish.append(sent)
        return wait

    def head_to_tok(t, src, dst):
        def copy(j, owner):
            return remote(
                src.at[cols(j), :], dst.at[:, cols(owner)],
                s["s_a2a"].at[t, j], s["r_a2a"].at[t, owner], (dp, j),
            )

        own = pltpu.make_async_copy(src.at[cols(me), :], dst.at[:, cols(me)], s["local"].at[t])

        def send(j):
            @pl.when(j != me)
            def _():
                copy(j, me).start()

            @pl.when(j == me)
            def _():
                own.start()

        def wait():
            def one(i, _):
                j = lax.rem(me + i, 16)
                copy(j, j).wait_recv()
                return 0

            own.wait()
            lax.fori_loop(1, 16, one, 0)

        def sent():
            def one(i, _):
                copy(lax.rem(me + i, 16), me).wait_send()
                return 0

            lax.fori_loop(1, 16, one, 0)

        finish.append(sent)
        return send, wait

    def spread(t, src_of, dst_of, index, device_of):
        def copy(j, owner):
            return remote(
                src_of(j), dst_of(owner), s["s_gate"].at[t, j], s["r_gate"].at[t, owner],
                device_of(j),
            )

        def start(i, _):
            copy(lax.rem(index + i, 16), index).start()
            return 0

        own = pltpu.make_async_copy(src_of(index), dst_of(index), s["local"].at[8 + t])
        own.start()
        lax.fori_loop(1, 16, start, 0)

        def wait():
            def one(i, _):
                j = lax.rem(index + i, 16)
                copy(j, j).wait_recv()
                return 0

            own.wait()
            lax.fori_loop(1, 16, one, 0)

        def sent():
            def one(i, _):
                copy(lax.rem(index + i, 16), index).wait_send()
                return 0

            lax.fori_loop(1, 16, one, 0)

        finish.append(sent)
        return wait

    weights = [(lift, s["liftf"], 64, 256), (outw, s["outf"], 32, 384)]
    z_hops = [at_z(1), at_z(7), at_z(2 + 4 * c)]
    along_z = []
    for n, (shard, full, height, width) in enumerate(weights):
        rows = pl.ds(pl.multiple_of(c * height, height), height)
        part = pl.ds(pl.multiple_of(y * width, 128), width)
        for i, device in enumerate(z_hops):
            along_z.append(
                go(shard.at[rows, part], full.at[zl, x, rows, part],
                   s["s_w"].at[n, i], s["r_w"].at[n, i], device).wait_recv
            )
        own = pltpu.make_async_copy(
            shard.at[rows, part], full.at[zl, x, rows, part], s["local"].at[12 + n]
        )
        own.start()
        along_z.append(own.wait)
    got_q = tok_to_head(0, q, s["qh"])
    got_k = tok_to_head(1, k, s["kh"])
    got_v = tok_to_head(2, v, s["vh"])
    got_gate = spread(
        0, lambda j: gate.at[:, cols(me)],
        lambda j: s["gcols"].at[pl.ds(pl.multiple_of(j * 16, 16), 16), :], dp,
        lambda j: (j, me),
    )
    got_emb = spread(1, lambda j: emb, lambda j: s["embs"].at[j], dp, lambda j: (j, me))

    wide = enc[...].astype(F32)
    centred = wide - jnp.mean(wide, axis=-1, keepdims=True)
    variance = jnp.mean(centred * centred, axis=-1, keepdims=True)
    normed = (centred * lax.rsqrt(variance + EPSILON) * gain[...] + bias[...]).astype(BF16)
    own_row, own_col = lax.shift_right_logical(trow[...], 7), lax.shift_right_logical(tcol[...], 7)
    before = lax.broadcasted_iota(jnp.int32, (TOK, TOK), 0) < lax.broadcasted_iota(
        jnp.int32, (TOK, TOK), 1
    )
    same = jnp.where((own_col == own_row) & before, 1.0, 0.0)
    slot = own_row.astype(F32) * 16.0 + jnp.sum(same, axis=0, keepdims=True)
    place = jnp.broadcast_to(((tcol[...] & 127) + 1).astype(F32), (TOK, 128)).astype(BF16)
    slots = lax.broadcasted_iota(jnp.int32, (256, TOK), 0).astype(F32)
    pick = jnp.where(slots == slot, 1.0, 0.0).astype(BF16)
    s["rows_send"][:, :ZD] = dot(pick, normed, ((1,), (0,))).astype(BF16)
    s["rows_send"][:, ZD:] = dot(pick, place, ((1,), (0,))).astype(BF16)

    def relay(j, owner):
        return remote(
            s["rows_send"].at[pl.ds(pl.multiple_of(j * 16, 16), 16), :],
            s["rows_got"].at[pl.ds(pl.multiple_of(owner * 16, 16), 16), :],
            s["s_rel"].at[j], s["r_rel"].at[owner], (dp, j),
        )

    def relay_start(i, _):
        relay(lax.rem(me + i, 16), me).start()
        return 0

    lax.fori_loop(1, 16, relay_start, 0)
    mine = pl.ds(pl.multiple_of(me * 16, 16), 16)
    relay_own = pltpu.make_async_copy(
        s["rows_send"].at[mine, :], s["rows_got"].at[mine, :], s["local"].at[14]
    )
    relay_own.start()

    def relay_sent():
        def one(i, _):
            relay(lax.rem(me + i, 16), me).wait_send()
            return 0

        lax.fori_loop(1, 16, one, 0)

    finish.append(relay_sent)

    for wait in along_z:
        wait()
    along_y = []
    for n, (_, full, height, width) in enumerate(weights):
        rows = pl.ds(pl.multiple_of(c * height, height), height)
        part = pl.ds(pl.multiple_of(y * width, 128), width)
        for i in range(1, 4):
            piece = full.at[:, x, rows, part]
            along_y.append(
                go(piece, piece, s["s_w"].at[n, 2 + i], s["r_w"].at[n, 2 + i], at_y(i))
            )
    for copy in along_y:
        copy.wait_recv()
    along_x, to_core = [], []

    def core_piece(n, i):
        _, full, height, _ = weights[n]
        piece = full.at[:, lax.rem(x + 4 - i, 4), pl.ds(pl.multiple_of(c * height, height), height), :]
        to_core.append(go(piece, piece, s["s_w"].at[n, 9 + i], s["r_w"].at[n, 9 + i], partner))

    for n, (_, full, height, _) in enumerate(weights):
        rows = pl.ds(pl.multiple_of(c * height, height), height)
        for i in range(1, 4):
            piece = full.at[:, x, rows, :]
            along_x.append(
                (n, i, go(piece, piece, s["s_w"].at[n, 5 + i], s["r_w"].at[n, 5 + i], at_x(i)))
            )
        core_piece(n, 0)

    got_gate()
    gating = dot(emb[...].astype(BF16), s["gcols"][...], ((1,), (0,)))[0:1]
    got_q()
    got_k()
    got_v()
    send_mix, got_mix = head_to_tok(3, s["gated"], s["mix_tok"])

    def forward(i, _):
        block = lax.rem(lax.div(me, 2) + i, LEN // QB)
        at = pl.ds(pl.multiple_of(block * QB, QB), QB)
        scores = dot(s["qh"][at, :], s["kh"][...], ((1,), (1,)))
        most = jnp.max(scores, axis=1, keepdims=True)
        shifted = jnp.exp2((scores - most) * LOG2)
        total = jnp.sum(shifted, axis=1, keepdims=True)
        mixed = dot(shifted.astype(BF16), s["vh"][...], ((1,), (0,))) / total
        s["o32"][at, :] = mixed
        s["gated"][at, :] = (gating * mixed.astype(BF16).astype(F32)).astype(BF16)
        level = jnp.broadcast_to(most * LOG2 + jnp.log2(total), (QB, 128))
        s["lse"][:, at] = jnp.transpose(level)[0:8]
        send_mix(2 * block)
        send_mix(2 * block + 1)
        return 0

    lax.fori_loop(0, LEN // QB, forward, 0)
    for n, i, copy in along_x:
        copy.wait_recv()
        core_piece(n, i)

    def relay_wait(i, _):
        j = lax.rem(me + i, 16)
        relay(j, j).wait_recv()
        return 0

    relay_own.wait()
    lax.fori_loop(1, 16, relay_wait, 0)
    tokens = lax.broadcasted_iota(jnp.int32, (256, TOK), 1).astype(F32) + 1.0
    placed = jnp.where(s["rows_got"][:, ZD : ZD + 1].astype(F32) == tokens, 1.0, 0.0).astype(BF16)
    target = dot(placed, s["rows_got"][:, :ZD], ((0,), (0,)))
    target_norm = jnp.sqrt(jnp.sum(target * target, axis=1, keepdims=True) + EPSILON)

    got_mix()
    hidden = (res[...].astype(F32) + s["mix_tok"][...].astype(F32)).astype(BF16)
    s["hid2"][0:TOK, :] = hidden
    pair = [
        go(s["hid2"].at[0:TOK, :], s["hid2"].at[TOK:, :],
           s["s_pair"].at[0], s["r_pair"].at[0], partner)
    ]
    for copy in to_core:
        copy.wait_recv()
    lifted = jnp.zeros((TOK, PH), F32)
    for i in range(4):
        lifted += dot(
            s["hid2"][0:TOK, i * 512 : (i + 1) * 512],
            s["liftf"][i].reshape(512, PH), ((1,), (0,)),
        )
    sigmoid = jax.nn.sigmoid(lifted)
    s["act2"][0:TOK, :] = (lifted * sigmoid).astype(BF16)
    slope = sigmoid * (1.0 + lifted * (1.0 - sigmoid))
    pair.append(
        go(s["act2"].at[0:TOK, :], s["act2"].at[TOK:, :],
           s["s_pair"].at[1], s["r_pair"].at[1], partner)
    )
    predicted = jnp.zeros((TOK, ZD), F32)
    for i in range(4):
        predicted += dot(
            s["act2"][0:TOK, i * 256 : (i + 1) * 256],
            s["outf"][i].reshape(256, ZD), ((1,), (0,)),
        )
    pred_norm = jnp.sqrt(jnp.sum(predicted * predicted, axis=1, keepdims=True) + EPSILON)
    both = pred_norm * target_norm
    cosine = jnp.sum(predicted * target, axis=1, keepdims=True) / both
    grad_pred = (
        (-1.0 * ZD) * (target / both - cosine * predicted / (pred_norm * pred_norm))
    ).astype(BF16)
    s["gpf"][0] = grad_pred[:, : ZD // 2]
    s["gpf"][1] = grad_pred[:, ZD // 2 :]
    pair.append(
        go(s["gpf"].at[1 - c], s["gp2"].at[TOK:, :], s["s_pair"].at[2], s["r_pair"].at[2], partner)
    )
    for i in range(4):
        at = slice(i * 256, (i + 1) * 256)
        grad_act = dot(grad_pred, s["outf"][i].reshape(256, ZD), ((1,), (1,)))
        s["glf"][i // 2, :, (i % 2) * 256 : (i % 2 + 1) * 256] = (
            grad_act * slope[:, at]
        ).astype(BF16)
    pair.append(
        go(s["glf"].at[1 - c], s["gl2"].at[TOK:, :], s["s_pair"].at[3], s["r_pair"].at[3], partner)
    )
    grad_lifted = jnp.concatenate([s["glf"][0], s["glf"][1]], axis=1)
    for i in range(4):
        s["ghs"][:, i * 512 : (i + 1) * 512] = dot(
            grad_lifted, s["liftf"][i].reshape(512, PH), ((1,), (1,))
        ).astype(BF16)
    got_grad = tok_to_head(4, s["ghs"], s["gh"])

    s["gp2"][0:TOK, :] = s["gpf"][c]
    s["gl2"][0:TOK, :] = s["glf"][c]
    for copy in pair:
        copy.wait_recv()

    def lift_part(i, _):
        s["gl_x"][lax.div(i, 4), lax.rem(i, 4)] = dot(
            s["hid2"][:, cols(i)], s["gl2"][...], ((0,), (0,))
        ).astype(BF16)
        return 0

    lax.fori_loop(0, 16, lift_part, 0)

    def out_part(i, _):
        done = dot(s["act2"][:, cols(i)], s["gp2"][...], ((0,), (0,))).astype(BF16)
        first = 2 * i
        s["go_x"][lax.div(first, 4), lax.rem(first, 4)] = done[:64]
        s["go_x"][lax.div(first, 4), lax.rem(first, 4) + 1] = done[64:]
        return 0

    lax.fori_loop(0, 8, out_part, 0)
    sums = []
    for n, (part, room) in enumerate([("gl_x", "rl_x"), ("go_x", "ro_x")]):
        for i in range(1, 4):
            sums.append(
                go(s[part].at[:, lax.rem(x + i, 4)], s[room].at[i - 1],
                   s["s_red"].at[n, i - 1], s["r_red"].at[n, i - 1], at_x(i))
            )

    got_grad()
    ones = jnp.ones((8, HD), F32)

    def prepare(i, total):
        at = pl.ds(pl.multiple_of(i * QB, QB), QB)
        grad = s["gh"][at, :].astype(F32)
        mixed = s["o32"][at, :]
        scaled = (gating * grad).astype(BF16)
        s["do"][at, :] = scaled
        s["drow"][:, at] = dot(
            ones, scaled.astype(F32) * mixed, ((1,), (1,)), lax.Precision.HIGHEST
        )
        product = grad * mixed.astype(BF16).astype(F32)
        return total + jnp.sum(product.reshape(QB // 8, 8, HD), axis=0)

    s["ggs"][...] = lax.fori_loop(0, LEN // QB, prepare, jnp.zeros((8, HD), F32))
    got_gg = spread(2, lambda j: s["ggs"], lambda j: s["ggall"].at[j], dp, lambda j: (j, me))
    s["dq32"][...] = jnp.zeros((LEN, HD), F32)
    send_dk, got_dk = head_to_tok(5, s["dkb"], dk)
    send_dv, got_dv = head_to_tok(6, s["dvb"], dv)
    send_dq, got_dq = head_to_tok(7, s["dqb"], dq)

    def backward(i, _):
        block = lax.rem(lax.div(me, 2) + i, LEN // KB)
        at = pl.ds(pl.multiple_of(block * KB, KB), KB)
        keys = s["kh"][at, :]
        scores = dot(keys, s["qh"][...], ((1,), (1,)))
        chances = jnp.exp2(scores * LOG2 - s["lse"][0:1, :])
        s["dvb"][at, :] = dot(chances.astype(BF16), s["do"][...], ((1,), (0,))).astype(BF16)
        grad_chances = dot(s["vh"][at, :], s["do"][...], ((1,), (1,)))
        grad_scores = (chances * (grad_chances - s["drow"][0:1, :])).astype(BF16)
        s["dkb"][at, :] = (dot(grad_scores, s["qh"][...], ((1,), (0,))) * SCALE).astype(BF16)
        for send in (send_dv, send_dk):
            send(2 * block)
            send(2 * block + 1)
        s["dq32"][...] += dot(grad_scores, keys, ((0,), (0,)))
        return 0

    lax.fori_loop(0, LEN // KB, backward, 0)
    s["dqb"][...] = (s["dq32"][...] * SCALE).astype(BF16)

    def send_queries(i, _):
        send_dq(lax.rem(me + i, 16))
        return 0

    lax.fori_loop(0, 16, send_queries, 0)

    got_emb()
    got_gg()
    s["gfull"][...] = dot(
        s["embs"][...].reshape(128, TEMB), s["ggall"][...].reshape(128, HD), ((0,), (0,)),
        lax.Precision.HIGHEST,
    )
    s["gsl"][...] = s["gfull"][pl.ds(pl.multiple_of(dp * 16, 16), 16), :]
    got_ggate = spread(
        3, lambda j: s["gsl"], lambda j: ggate.at[:, cols(j)], me, lambda j: (dp, j)
    )

    for copy in sums:
        copy.wait_recv()
    s["gl_y"][...] = (s["gl_x"][:, x].astype(F32) + s["rl_x"][0].astype(F32)
                      + s["rl_x"][1].astype(F32) + s["rl_x"][2].astype(F32)).astype(BF16)
    s["go_y"][...] = (s["go_x"][:, x].astype(F32) + s["ro_x"][0].astype(F32)
                      + s["ro_x"][1].astype(F32) + s["ro_x"][2].astype(F32)).astype(BF16)
    sums = []
    reduced = [("gl_y", "rl_y", 32), ("go_y", "ro_y", 16)]
    for n, (part, room, height) in enumerate(reduced):
        for i in range(1, 4):
            rows = pl.ds(pl.multiple_of(lax.rem(y + i, 4) * height, height), height)
            sums.append(
                go(s[part].at[:, rows, :], s[room].at[i - 1],
                   s["s_red"].at[n, 2 + i], s["r_red"].at[n, 2 + i], at_y(i))
            )
    for copy in sums:
        copy.wait_recv()
    for (part, room, height), nxt in zip(reduced, ("gl_z", "go_z")):
        rows = pl.ds(pl.multiple_of(y * height, height), height)
        s[nxt][...] = (s[part][:, rows, :].astype(F32) + s[room][0].astype(F32)
                       + s[room][1].astype(F32) + s[room][2].astype(F32)).astype(BF16)
    sums = []
    for n, (part, room) in enumerate([("gl_z", "rl_z"), ("go_z", "ro_z")]):
        for i in range(1, 8):
            sums.append(
                go(s[part].at[lax.rem(z + i, 4)], s[room].at[i - 1],
                   s["s_red"].at[n, 5 + i], s["r_red"].at[n, 5 + i], at_z(i))
            )
    for copy in sums:
        copy.wait_recv()
    sums = []
    final = [
        ("gl_z", "rl_z", "pl_f", glift, 32, PH // 2),
        ("go_z", "ro_z", "po_f", gout, 16, ZD // 2),
    ]
    for n, (part, room, piece, whole, height, width) in enumerate(final):
        total = s[part][zl].astype(F32)
        for i in range(7):
            total += s[room][i].astype(F32)
        s[piece][...] = total
        to = whole.at[
            pl.ds(pl.multiple_of(y * height, height), height),
            pl.ds(pl.multiple_of(c * width, 128), width),
        ]
        own = pltpu.make_async_copy(s[piece], to, s["local"].at[15 + n])
        own.start()
        finish.append(own.wait)
        for i in range(1, 8):
            sums.append(
                go(s[piece], to, s["s_red"].at[n, 12 + i], s["r_red"].at[n, 12 + i], at_yc(i))
            )
    got_ggate()
    for copy in sums:
        copy.wait_recv()
    got_dk()
    got_dv()
    got_dq()
    for wait in finish:
        wait()


def embed_time(timestep):
    half_width = TEMB // 2
    frequency = jnp.exp(-math.log(10000.0) * jnp.arange(half_width).astype(F32) / half_width)
    angles = timestep.astype(F32)[:, None] * frequency[None, :]
    return jnp.concatenate([jnp.cos(angles), jnp.sin(angles)], axis=1).astype(BF16)


def shards(
    queries,
    key_states,
    value_states,
    residual,
    enc_hidden,
    enc_gain,
    enc_bias,
    feature_target,
    timestep,
    gate_weight,
    lift_weight,
    out_weight,
):
    embedded = jnp.broadcast_to(embed_time(timestep).astype(F32), (8, TEMB))
    anywhere = pl.BlockSpec(memory_space=pl.ANY)
    near = pl.BlockSpec(memory_space=pltpu.VMEM)
    tok = jax.ShapeDtypeStruct((TOK, FEAT), BF16)
    outs = pl.pallas_call(
        step_kernel,
        out_shape=(
            tok, tok, tok,
            jax.ShapeDtypeStruct((16, FEAT), F32),
            jax.ShapeDtypeStruct((128, PH), F32),
            jax.ShapeDtypeStruct((64, ZD), F32),
        ),
        in_specs=[anywhere] * 3 + [near] * 7 + [anywhere] * 3,
        out_specs=(anywhere,) * 6,
        scratch_shapes=list(SCRATCH.values()),
        compiler_params=pltpu.CompilerParams(
            collective_id=0, has_side_effects=True, vmem_limit_bytes=60 << 20
        ),
        name="repa_step",
    )(
        queries[0], key_states[0], value_states[0], residual[0], enc_hidden[0],
        enc_gain[None], enc_bias[None], feature_target, feature_target.reshape(TOK, 1),
        embedded, gate_weight, lift_weight, out_weight,
    )
    d_queries, d_keys, d_values, grad_gate, grad_lift, grad_out = outs
    return (d_queries[None], d_keys[None], d_values[None], grad_gate, grad_lift, grad_out)


def solution(mesh):
    tokens = P("dp", "seq", None)
    rows = P("dp", None)
    in_specs = (tokens,) * 5 + (P(), P(), P("dp", "seq"), P("dp"), rows, rows, rows)
    out_specs = (tokens,) * 3 + (rows,) * 3
    return jax.shard_map(
        shards, mesh=mesh, in_specs=in_specs, out_specs=out_specs, check_vma=False
    )
```

```python
import functools
import math

import jax
import jax.numpy as jnp
from jax import lax
from jax.experimental import pallas as pl
from jax.experimental.pallas import tpu as pltpu
from jax.sharding import PartitionSpec as P

HD = 128
ZD = 1536
PH = 1024
FEAT = 2048
TEMB = 256
LEN = 2048
TOK = 128
EPSILON = 1e-06
SCALE = HD ** (-0.5)
LOG2 = SCALE * math.log2(math.e)
QB = 256
KB = 256
MESH = pl.DeviceIdType.MESH
F32 = jnp.float32
BF16 = jnp.bfloat16

SCRATCH = dict(
    qh=pltpu.VMEM((LEN, HD), BF16),
    kh=pltpu.VMEM((LEN, HD), BF16),
    vh=pltpu.VMEM((LEN, HD), BF16),
    gcols=pltpu.VMEM((TEMB, HD), BF16),
    emb=pltpu.VMEM((8, TEMB), F32),
    embs=pltpu.VMEM((16, 8, TEMB), F32),
    rows_send=pltpu.VMEM((256, ZD + 128), BF16),
    rows_got=pltpu.VMEM((256, ZD + 128), BF16),
    liftf=pltpu.VMEM((4, 4, 128, PH), BF16),
    outf=pltpu.VMEM((4, 4, 64, ZD), BF16),
    o32=pltpu.VMEM((LEN, HD), F32),
    lse=pltpu.VMEM((8, LEN), F32),
    gated=pltpu.VMEM((LEN, HD), BF16),
    mix_tok=pltpu.VMEM((TOK, FEAT), BF16),
    hid2=pltpu.VMEM((2 * TOK, FEAT), BF16),
    act2=pltpu.VMEM((2 * TOK, PH), BF16),
    gpf=pltpu.VMEM((2, TOK, ZD // 2), BF16),
    gp2=pltpu.VMEM((2 * TOK, ZD // 2), BF16),
    glf=pltpu.VMEM((2, TOK, PH // 2), BF16),
    gl2=pltpu.VMEM((2 * TOK, PH // 2), BF16),
    ghs=pltpu.VMEM((TOK, FEAT), BF16),
    gh=pltpu.VMEM((LEN, HD), BF16),
    do=pltpu.VMEM((LEN, HD), BF16),
    drow=pltpu.VMEM((8, LEN), F32),
    dq32=pltpu.VMEM((LEN, HD), F32),
    dqb=pltpu.VMEM((LEN, HD), BF16),
    dkb=pltpu.VMEM((LEN, HD), BF16),
    dvb=pltpu.VMEM((LEN, HD), BF16),
    ggs=pltpu.VMEM((8, HD), F32),
    ggall=pltpu.VMEM((16, 8, HD), F32),
    gfull=pltpu.VMEM((TEMB, HD), F32),
    gsl=pltpu.VMEM((16, HD), F32),
    gl_x=pltpu.VMEM((4, 4, 128, PH // 2), BF16),
    go_x=pltpu.VMEM((4, 4, 64, ZD // 2), BF16),
    rl_x=pltpu.VMEM((3, 4, 128, PH // 2), BF16),
    ro_y=pltpu.VMEM((3, 4, 4, 16, ZD // 2), BF16),
    gl_y=pltpu.VMEM((4, 128, PH // 2), BF16),
    go_y=pltpu.VMEM((4, 4, 16, ZD // 2), BF16),
    rl_y=pltpu.VMEM((3, 4, 32, PH // 2), BF16),
    ro_x=pltpu.VMEM((3, 4, 16, ZD // 2), BF16),
    gl_z=pltpu.VMEM((4, 32, PH // 2), BF16),
    go_z=pltpu.VMEM((4, 16, ZD // 2), BF16),
    rl_z=pltpu.VMEM((7, 32, PH // 2), BF16),
    ro_z=pltpu.VMEM((7, 16, ZD // 2), BF16),
    pl_f=pltpu.VMEM((32, PH // 2), F32),
    po_f=pltpu.VMEM((16, ZD // 2), F32),
    s_a2a=pltpu.SemaphoreType.DMA((8, 16)),
    r_a2a=pltpu.SemaphoreType.DMA((8, 16)),
    s_rel=pltpu.SemaphoreType.DMA((16,)),
    r_rel=pltpu.SemaphoreType.DMA((16,)),
    s_gate=pltpu.SemaphoreType.DMA((4, 16)),
    r_gate=pltpu.SemaphoreType.DMA((4, 16)),
    s_w=pltpu.SemaphoreType.DMA((2, 13)),
    r_w=pltpu.SemaphoreType.DMA((2, 13)),
    s_pair=pltpu.SemaphoreType.DMA((4,)),
    r_pair=pltpu.SemaphoreType.DMA((4,)),
    s_red=pltpu.SemaphoreType.DMA((2, 20)),
    r_red=pltpu.SemaphoreType.DMA((2, 20)),
    local=pltpu.SemaphoreType.DMA((20,)),
)
NAMES = list(SCRATCH)


def dot(a, b, dims, precision=None):
    return lax.dot_general(
        a, b, (dims, ((), ())), precision=precision, preferred_element_type=F32
    )


def step_kernel(*refs):
    q, k, v, res, enc, gain, bias, trow, when, gate, lift, outw = refs[:12]
    dq, dk, dv, ggate, glift, gout = refs[12:18]
    s = dict(zip(NAMES, refs[18:]))
    dp, me = lax.axis_index("dp"), lax.axis_index("seq")
    zl, x = lax.div(dp, 4), lax.rem(dp, 4)
    zh, yc = lax.div(me, 8), lax.rem(me, 8)
    y, c = lax.div(yc, 2), lax.rem(yc, 2)
    z = zh * 4 + zl
    partner = (dp, me + 1 - 2 * c)

    def at_x(i):
        return (zl * 4 + lax.rem(x + i, 4), me)

    def at_y(i):
        return (dp, zh * 8 + lax.rem(y + i, 4) * 2 + c)

    def at_z(i):
        to = lax.rem(z + i, 8)
        return (lax.rem(to, 4) * 4 + x, lax.div(to, 4) * 8 + yc)

    def at_yc(i):
        return (dp, zh * 8 + lax.rem(yc + i, 8))

    def cols(j):
        return pl.ds(pl.multiple_of(j * 128, 128), 128)

    def remote(src, dst, send, recv, device):
        return pltpu.make_async_remote_copy(
            src_ref=src, dst_ref=dst, send_sem=send, recv_sem=recv,
            device_id=device, device_id_type=MESH,
        )

    finish = []

    def go(*copy):
        made = remote(*copy)
        made.start()
        finish.append(made.wait_send)
        return made

    half = TEMB // 2
    index = lax.broadcasted_iota(jnp.int32, (8, half), 1).astype(F32)
    angles = when[0].astype(F32) * jnp.exp(-math.log(10000.0) * index / half)
    s["emb"][:, :half] = jnp.cos(angles).astype(BF16).astype(F32)
    s["emb"][:, half:] = jnp.sin(angles).astype(BF16).astype(F32)

    barrier = pltpu.get_barrier_semaphore()

    def greet(i, _):
        pl.semaphore_signal(barrier, 1, device_id=(dp, lax.rem(me + i, 16)), device_id_type=MESH)
        pl.semaphore_signal(barrier, 1, device_id=(lax.rem(dp + i, 16), me), device_id_type=MESH)
        return 0

    lax.fori_loop(1, 16, greet, 0)
    for i in range(1, 4):
        other = (lax.rem(zl + i, 4) * 4 + x, (1 - zh) * 8 + yc)
        pl.semaphore_signal(barrier, 1, device_id=other, device_id_type=MESH)
    pl.semaphore_wait(barrier, 33)

    def tok_to_head(t, src, dst):
        def copy(j, owner):
            return remote(
                src.at[:, cols(j)], dst.at[cols(owner), :],
                s["s_a2a"].at[t, j], s["r_a2a"].at[t, owner], (dp, j),
            )

        def start(i, _):
            copy(lax.rem(me + i, 16), me).start()
            return 0

        own = pltpu.make_async_copy(src.at[:, cols(me)], dst.at[cols(me), :], s["local"].at[t])
        own.start()
        lax.fori_loop(1, 16, start, 0)

        def wait():
            def one(i, _):
                j = lax.rem(me + i, 16)
                copy(j, j).wait_recv()
                return 0

            own.wait()
            lax.fori_loop(1, 16, one, 0)

        def sent():
            def one(i, _):
                copy(lax.rem(me + i, 16), me).wait_send()
                return 0

            lax.fori_loop(1, 16, one, 0)

        finish.append(sent)
        return wait

    def head_to_tok(t, src, dst):
        def copy(j, owner):
            return remote(
                src.at[cols(j), :], dst.at[:, cols(owner)],
                s["s_a2a"].at[t, j], s["r_a2a"].at[t, owner], (dp, j),
            )

        own = pltpu.make_async_copy(src.at[cols(me), :], dst.at[:, cols(me)], s["local"].at[t])

        def send(j):
            @pl.when(j != me)
            def _():
                copy(j, me).start()

            @pl.when(j == me)
            def _():
                own.start()

        def wait():
            def one(i, _):
                j = lax.rem(me + i, 16)
                copy(j, j).wait_recv()
                return 0

            own.wait()
            lax.fori_loop(1, 16, one, 0)

        def sent():
            def one(i, _):
                copy(lax.rem(me + i, 16), me).wait_send()
                return 0

            lax.fori_loop(1, 16, one, 0)

        finish.append(sent)
        return send, wait

    def spread(t, src_of, dst_of, index, device_of):
        def copy(j, owner):
            return remote(
                src_of(j), dst_of(owner), s["s_gate"].at[t, j], s["r_gate"].at[t, owner],
                device_of(j),
            )

        def start(i, _):
            copy(lax.rem(index + i, 16), index).start()
            return 0

        own = pltpu.make_async_copy(src_of(index), dst_of(index), s["local"].at[8 + t])
        own.start()
        lax.fori_loop(1, 16, start, 0)

        def wait():
            def one(i, _):
                j = lax.rem(index + i, 16)
                copy(j, j).wait_recv()
                return 0

            own.wait()
            lax.fori_loop(1, 16, one, 0)

        def sent():
            def one(i, _):
                copy(lax.rem(index + i, 16), index).wait_send()
                return 0

            lax.fori_loop(1, 16, one, 0)

        finish.append(sent)
        return wait

    weights = [(lift, s["liftf"], 64, 256), (outw, s["outf"], 32, 384)]
    z_hops = [at_z(1), at_z(7), at_z(2 + 4 * c)]
    along_z = []
    for n, (shard, full, height, width) in enumerate(weights):
        rows = pl.ds(pl.multiple_of(c * height, height), height)
        part = pl.ds(pl.multiple_of(y * width, 128), width)
        for i, device in enumerate(z_hops):
            along_z.append(
                go(shard.at[rows, part], full.at[zl, x, rows, part],
                   s["s_w"].at[n, i], s["r_w"].at[n, i], device).wait_recv
            )
        own = pltpu.make_async_copy(
            shard.at[rows, part], full.at[zl, x, rows, part], s["local"].at[12 + n]
        )
        own.start()
        along_z.append(own.wait)
    got_q = tok_to_head(0, q, s["qh"])
    got_k = tok_to_head(1, k, s["kh"])
    got_v = tok_to_head(2, v, s["vh"])
    got_gate = spread(
        0, lambda j: gate.at[:, cols(me)],
        lambda j: s["gcols"].at[pl.ds(pl.multiple_of(j * 16, 16), 16), :], dp,
        lambda j: (j, me),
    )
    got_emb = spread(1, lambda j: s["emb"], lambda j: s["embs"].at[j], dp, lambda j: (j, me))

    wide = enc[...].astype(F32)
    centred = wide - jnp.mean(wide, axis=-1, keepdims=True)
    variance = jnp.mean(centred * centred, axis=-1, keepdims=True)
    normed = (centred * lax.rsqrt(variance + EPSILON) * gain[...][None] + bias[...][None]).astype(BF16)
    tcol = jnp.transpose(jnp.broadcast_to(trow[...], (TOK, TOK)))
    own_row, own_col = lax.shift_right_logical(trow[...], 7), lax.shift_right_logical(tcol, 7)
    before = lax.broadcasted_iota(jnp.int32, (TOK, TOK), 0) < lax.broadcasted_iota(
        jnp.int32, (TOK, TOK), 1
    )
    same = jnp.where((own_col == own_row) & before, 1.0, 0.0)
    slot = own_row.astype(F32) * 16.0 + jnp.sum(same, axis=0, keepdims=True)
    place = ((tcol & 127) + 1).astype(F32).astype(BF16)
    slots = lax.broadcasted_iota(jnp.int32, (256, TOK), 0).astype(F32)
    pick = jnp.where(slots == slot, 1.0, 0.0).astype(BF16)
    s["rows_send"][:, :ZD] = dot(pick, normed, ((1,), (0,))).astype(BF16)
    s["rows_send"][:, ZD:] = dot(pick, place, ((1,), (0,))).astype(BF16)

    def relay(j, owner):
        return remote(
            s["rows_send"].at[pl.ds(pl.multiple_of(j * 16, 16), 16), :],
            s["rows_got"].at[pl.ds(pl.multiple_of(owner * 16, 16), 16), :],
            s["s_rel"].at[j], s["r_rel"].at[owner], (dp, j),
        )

    def relay_start(i, _):
        relay(lax.rem(me + i, 16), me).start()
        return 0

    def relay_sent():
        def one(i, _):
            relay(lax.rem(me + i, 16), me).wait_send()
            return 0

        lax.fori_loop(1, 16, one, 0)

    finish.append(relay_sent)

    for wait in along_z:
        wait()
    along_y = []
    for n, (_, full, height, width) in enumerate(weights):
        rows = pl.ds(pl.multiple_of(c * height, height), height)
        part = pl.ds(pl.multiple_of(y * width, 128), width)
        for i in range(1, 4):
            piece = full.at[:, x, rows, part]
            along_y.append(
                go(piece, piece, s["s_w"].at[n, 2 + i], s["r_w"].at[n, 2 + i], at_y(i))
            )
    for copy in along_y:
        copy.wait_recv()
    along_x, to_core = [], []

    def core_piece(n, i):
        _, full, height, _ = weights[n]
        piece = full.at[:, lax.rem(x + 4 - i, 4), pl.ds(pl.multiple_of(c * height, height), height), :]
        to_core.append(go(piece, piece, s["s_w"].at[n, 9 + i], s["r_w"].at[n, 9 + i], partner))

    for n, (_, full, height, _) in enumerate(weights):
        rows = pl.ds(pl.multiple_of(c * height, height), height)
        for i in range(1, 4):
            piece = full.at[:, x, rows, :]
            along_x.append(
                (n, i, go(piece, piece, s["s_w"].at[n, 5 + i], s["r_w"].at[n, 5 + i], at_x(i)))
            )
        core_piece(n, 0)

    got_gate()
    gating = dot(s["emb"][...].astype(BF16), s["gcols"][...], ((1,), (0,)))[0:1]
    got_q()
    got_k()
    got_v()
    lax.fori_loop(1, 16, relay_start, 0)
    mine = pl.ds(pl.multiple_of(me * 16, 16), 16)
    relay_own = pltpu.make_async_copy(
        s["rows_send"].at[mine, :], s["rows_got"].at[mine, :], s["local"].at[14]
    )
    relay_own.start()

    send_mix, got_mix = head_to_tok(3, s["gated"], s["mix_tok"])

    def forward(i, _):
        block = lax.rem(lax.div(me, 2) + i, LEN // QB)
        at = pl.ds(pl.multiple_of(block * QB, QB), QB)
        scores = dot(s["qh"][at, :], s["kh"][...], ((1,), (1,)))
        most = jnp.max(scores, axis=1, keepdims=True)
        shifted = jnp.exp2((scores - most) * LOG2)
        weight = jnp.sum(shifted, axis=1, keepdims=True)
        mixed = dot(shifted.astype(BF16), s["vh"][...], ((1,), (0,))) / weight
        s["o32"][at, :] = mixed
        s["gated"][at, :] = (gating * mixed.astype(BF16).astype(F32)).astype(BF16)
        level = jnp.broadcast_to(most * LOG2 + jnp.log2(weight), (QB, 128))
        s["lse"][:, at] = jnp.transpose(level)[0:8]
        send_mix(2 * block)
        send_mix(2 * block + 1)
        return 0

    lax.fori_loop(0, LEN // QB, forward, 0)
    for n, i, copy in along_x:
        copy.wait_recv()
        core_piece(n, i)

    def relay_wait(i, _):
        j = lax.rem(me + i, 16)
        relay(j, j).wait_recv()
        return 0

    relay_own.wait()
    lax.fori_loop(1, 16, relay_wait, 0)
    tokens = lax.broadcasted_iota(jnp.int32, (256, TOK), 1).astype(F32) + 1.0
    placed = jnp.where(s["rows_got"][:, ZD : ZD + 1].astype(F32) == tokens, 1.0, 0.0).astype(BF16)
    target = dot(placed, s["rows_got"][:, :ZD], ((0,), (0,)))
    target_norm = jnp.sqrt(jnp.sum(target * target, axis=1, keepdims=True) + EPSILON)

    got_mix()
    hidden = (res[...].astype(F32) + s["mix_tok"][...].astype(F32)).astype(BF16)
    s["hid2"][0:TOK, :] = hidden
    pair = [
        go(s["hid2"].at[0:TOK, :], s["hid2"].at[TOK:, :],
           s["s_pair"].at[0], s["r_pair"].at[0], partner)
    ]
    for copy in to_core:
        copy.wait_recv()
    lifted = jnp.zeros((TOK, PH), F32)
    for i in range(4):
        lifted += dot(
            s["hid2"][0:TOK, i * 512 : (i + 1) * 512],
            s["liftf"][i].reshape(512, PH), ((1,), (0,)),
        )
    sigmoid = jax.nn.sigmoid(lifted)
    s["act2"][0:TOK, :] = (lifted * sigmoid).astype(BF16)
    slope = sigmoid * (1.0 + lifted * (1.0 - sigmoid))
    pair.append(
        go(s["act2"].at[0:TOK, :], s["act2"].at[TOK:, :],
           s["s_pair"].at[1], s["r_pair"].at[1], partner)
    )
    predicted = jnp.zeros((TOK, ZD), F32)
    for i in range(4):
        predicted += dot(
            s["act2"][0:TOK, i * 256 : (i + 1) * 256],
            s["outf"][i].reshape(256, ZD), ((1,), (0,)),
        )
    pred_norm = jnp.sqrt(jnp.sum(predicted * predicted, axis=1, keepdims=True) + EPSILON)
    both = pred_norm * target_norm
    cosine = jnp.sum(predicted * target, axis=1, keepdims=True) / both
    grad_pred = (
        (-1.0 * ZD) * (target / both - cosine * predicted / (pred_norm * pred_norm))
    ).astype(BF16)
    s["gpf"][0] = grad_pred[:, : ZD // 2]
    s["gpf"][1] = grad_pred[:, ZD // 2 :]
    pair.append(
        go(s["gpf"].at[1 - c], s["gp2"].at[TOK:, :], s["s_pair"].at[2], s["r_pair"].at[2], partner)
    )
    for i in range(4):
        at = slice(i * 256, (i + 1) * 256)
        grad_act = dot(grad_pred, s["outf"][i].reshape(256, ZD), ((1,), (1,)))
        s["glf"][i // 2, :, (i % 2) * 256 : (i % 2 + 1) * 256] = (
            grad_act * slope[:, at]
        ).astype(BF16)
    pair.append(
        go(s["glf"].at[1 - c], s["gl2"].at[TOK:, :], s["s_pair"].at[3], s["r_pair"].at[3], partner)
    )
    grad_lifted = jnp.concatenate([s["glf"][0], s["glf"][1]], axis=1)
    for i in range(4):
        s["ghs"][:, i * 512 : (i + 1) * 512] = dot(
            grad_lifted, s["liftf"][i].reshape(512, PH), ((1,), (1,))
        ).astype(BF16)
    got_grad = tok_to_head(4, s["ghs"], s["gh"])

    s["gp2"][0:TOK, :] = s["gpf"][c]
    s["gl2"][0:TOK, :] = s["glf"][c]
    for copy in pair:
        copy.wait_recv()

    def lift_part(i, _):
        s["gl_x"][lax.div(i, 4), lax.rem(i, 4)] = dot(
            s["hid2"][:, cols(i)], s["gl2"][...], ((0,), (0,))
        ).astype(BF16)
        return 0

    lax.fori_loop(0, 16, lift_part, 0)

    def out_part(i, _):
        done = dot(s["act2"][:, cols(i)], s["gp2"][...], ((0,), (0,))).astype(BF16)
        first = 2 * i
        s["go_x"][lax.div(first, 4), lax.rem(first, 4)] = done[:64]
        s["go_x"][lax.div(first, 4), lax.rem(first, 4) + 1] = done[64:]
        return 0

    lax.fori_loop(0, 8, out_part, 0)
    sums = []
    for i in range(1, 4):
        rows = pl.ds(pl.multiple_of(lax.rem(y + i, 4) * 16, 16), 16)
        sums.append(
            go(s["gl_x"].at[:, lax.rem(x + i, 4)], s["rl_x"].at[i - 1],
               s["s_red"].at[0, i - 1], s["r_red"].at[0, i - 1], at_x(i))
        )
        sums.append(
            go(s["go_x"].at[:, :, rows, :], s["ro_y"].at[i - 1],
               s["s_red"].at[1, i - 1], s["r_red"].at[1, i - 1], at_y(i))
        )

    def total(own, room):
        added = own.astype(F32)
        for i in range(room.shape[0]):
            added += room[i].astype(F32)
        return added

    got_grad()
    ones = jnp.ones((8, HD), F32)

    def prepare(i, partial):
        at = pl.ds(pl.multiple_of(i * QB, QB), QB)
        grad = s["gh"][at, :].astype(F32)
        mixed = s["o32"][at, :]
        scaled = (gating * grad).astype(BF16)
        s["do"][at, :] = scaled
        s["drow"][:, at] = dot(
            ones, scaled.astype(F32) * mixed, ((1,), (1,)), lax.Precision.HIGHEST
        )
        product = grad * mixed.astype(BF16).astype(F32)
        return partial + jnp.sum(product.reshape(QB // 8, 8, HD), axis=0)

    s["ggs"][...] = lax.fori_loop(0, LEN // QB, prepare, jnp.zeros((8, HD), F32))
    got_gg = spread(2, lambda j: s["ggs"], lambda j: s["ggall"].at[j], dp, lambda j: (j, me))
    s["dq32"][...] = jnp.zeros((LEN, HD), F32)
    send_dk, got_dk = head_to_tok(5, s["dkb"], dk)
    send_dv, got_dv = head_to_tok(6, s["dvb"], dv)
    send_dq, got_dq = head_to_tok(7, s["dqb"], dq)

    def backward(i, _):
        block = lax.rem(lax.div(me, 2) + i, LEN // KB)
        at = pl.ds(pl.multiple_of(block * KB, KB), KB)
        keys = s["kh"][at, :]
        scores = dot(keys, s["qh"][...], ((1,), (1,)))
        chances = jnp.exp2(scores * LOG2 - s["lse"][0:1, :])
        s["dvb"][at, :] = dot(chances.astype(BF16), s["do"][...], ((1,), (0,))).astype(BF16)
        grad_chances = dot(s["vh"][at, :], s["do"][...], ((1,), (1,)))
        grad_scores = (chances * (grad_chances - s["drow"][0:1, :])).astype(BF16)
        s["dkb"][at, :] = (dot(grad_scores, s["qh"][...], ((1,), (0,))) * SCALE).astype(BF16)
        for send in (send_dv, send_dk):
            send(2 * block)
            send(2 * block + 1)
        s["dq32"][...] += dot(grad_scores, keys, ((0,), (0,)))
        return 0

    lax.fori_loop(0, LEN // KB // 2, backward, 0)

    for copy in sums:
        copy.wait_recv()
    s["gl_y"][...] = total(s["gl_x"][:, x], s["rl_x"]).astype(BF16)
    y_rows = pl.ds(pl.multiple_of(y * 16, 16), 16)
    s["go_y"][...] = total(s["go_x"][:, :, y_rows, :], s["ro_y"]).astype(BF16)
    sums = []
    for i in range(1, 4):
        rows = pl.ds(pl.multiple_of(lax.rem(y + i, 4) * 32, 32), 32)
        sums.append(
            go(s["gl_y"].at[:, rows, :], s["rl_y"].at[i - 1],
               s["s_red"].at[0, 2 + i], s["r_red"].at[0, 2 + i], at_y(i))
        )
        sums.append(
            go(s["go_y"].at[:, lax.rem(x + i, 4)], s["ro_x"].at[i - 1],
               s["s_red"].at[1, 2 + i], s["r_red"].at[1, 2 + i], at_x(i))
        )
    lax.fori_loop(LEN // KB // 2, LEN // KB, backward, 0)
    s["dqb"][...] = (s["dq32"][...] * SCALE).astype(BF16)

    def send_queries(i, _):
        send_dq(lax.rem(me + i, 16))
        return 0

    lax.fori_loop(0, 16, send_queries, 0)

    for copy in sums:
        copy.wait_recv()
    y_rows = pl.ds(pl.multiple_of(y * 32, 32), 32)
    s["gl_z"][...] = total(s["gl_y"][:, y_rows, :], s["rl_y"]).astype(BF16)
    s["go_z"][...] = total(s["go_y"][:, x], s["ro_x"]).astype(BF16)
    sums = []
    for n, (part, room) in enumerate([("gl_z", "rl_z"), ("go_z", "ro_z")]):
        for i in range(1, 8):
            sums.append(
                go(s[part].at[lax.rem(z + i, 4)], s[room].at[i - 1],
                   s["s_red"].at[n, 5 + i], s["r_red"].at[n, 5 + i], at_z(i))
            )

    got_emb()
    got_gg()
    s["gfull"][...] = dot(
        s["embs"][...].reshape(128, TEMB), s["ggall"][...].reshape(128, HD), ((0,), (0,)),
        lax.Precision.HIGHEST,
    )
    s["gsl"][...] = s["gfull"][pl.ds(pl.multiple_of(dp * 16, 16), 16), :]
    got_ggate = spread(
        3, lambda j: s["gsl"], lambda j: ggate.at[:, cols(j)], me, lambda j: (dp, j)
    )

    for copy in sums:
        copy.wait_recv()
    sums = []
    final = [
        ("gl_z", "rl_z", "pl_f", glift, 32, PH // 2),
        ("go_z", "ro_z", "po_f", gout, 16, ZD // 2),
    ]
    for n, (part, room, piece, whole, height, width) in enumerate(final):
        s[piece][...] = total(s[part][zl], s[room])
        to = whole.at[
            pl.ds(pl.multiple_of(y * height, height), height),
            pl.ds(pl.multiple_of(c * width, 128), width),
        ]
        own = pltpu.make_async_copy(s[piece], to, s["local"].at[15 + n])
        own.start()
        finish.append(own.wait)
        for i in range(1, 8):
            sums.append(
                go(s[piece], to, s["s_red"].at[n, 12 + i], s["r_red"].at[n, 12 + i], at_yc(i))
            )
    got_ggate()
    for copy in sums:
        copy.wait_recv()
    got_dk()
    got_dv()
    got_dq()
    for wait in finish:
        wait()


def copy_kernel(*refs):
    sems = refs[-1]
    copies = [
        pltpu.make_async_copy(refs[i], refs[6 + i], sems.at[i]) for i in range(6)
    ]
    for copy in copies:
        copy.start()
    for copy in copies:
        copy.wait()


def shards(
    queries,
    key_states,
    value_states,
    residual,
    enc_hidden,
    enc_gain,
    enc_bias,
    feature_target,
    timestep,
    gate_weight,
    lift_weight,
    out_weight,
):
    anywhere = pl.BlockSpec(memory_space=pl.ANY)
    near = pl.BlockSpec(memory_space=pltpu.VMEM)
    tok = jax.ShapeDtypeStruct((TOK, FEAT), BF16)
    out_shape = (
        tok, tok, tok,
        jax.ShapeDtypeStruct((16, FEAT), F32),
        jax.ShapeDtypeStruct((128, PH), F32),
        jax.ShapeDtypeStruct((64, ZD), F32),
    )
    outs = pl.pallas_call(
        step_kernel,
        out_shape=out_shape,
        in_specs=[anywhere] * 3 + [near] * 5 + [pl.BlockSpec(memory_space=pltpu.SMEM)]
        + [anywhere] * 3,
        out_specs=(anywhere,) * 6,
        scratch_shapes=list(SCRATCH.values()),
        compiler_params=pltpu.CompilerParams(
            collective_id=0, has_side_effects=True, vmem_limit_bytes=60 << 20
        ),
        name="repa_step",
    )(
        queries[0], key_states[0], value_states[0], residual[0], enc_hidden[0],
        enc_gain, enc_bias, feature_target, timestep, gate_weight, lift_weight, out_weight,
    )
    d_queries, d_keys, d_values, grad_gate, grad_lift, grad_out = pl.pallas_call(
        copy_kernel,
        out_shape=out_shape,
        in_specs=[anywhere] * 6,
        out_specs=(anywhere,) * 6,
        scratch_shapes=[pltpu.SemaphoreType.DMA((6,))],
        name="hand_out",
    )(*outs)
    return (d_queries[None], d_keys[None], d_values[None], grad_gate, grad_lift, grad_out)


def solution(mesh):
    tokens = P("dp", "seq", None)
    rows = P("dp", None)
    in_specs = (tokens,) * 5 + (P(), P(), P("dp", "seq"), P("dp"), rows, rows, rows)
    out_specs = (tokens,) * 3 + (rows,) * 3
    return jax.shard_map(
        shards, mesh=mesh, in_specs=in_specs, out_specs=out_specs, check_vma=False
    )
```

```python
import functools
import math

import jax
import jax.numpy as jnp
from jax import lax
from jax.experimental import pallas as pl
from jax.experimental.pallas import tpu as pltpu
from jax.sharding import PartitionSpec as P

HD = 128
ZD = 1536
PH = 1024
FEAT = 2048
TEMB = 256
LEN = 2048
TOK = 128
EPSILON = 1e-06
SCALE = HD ** (-0.5)
LOG2 = SCALE * math.log2(math.e)
QB = 256
KB = 256
EARLY = 6
MESH = pl.DeviceIdType.MESH
F32 = jnp.float32
BF16 = jnp.bfloat16

SCRATCH = dict(
    qh=pltpu.VMEM((LEN, HD), BF16),
    kh=pltpu.VMEM((LEN, HD), BF16),
    vh=pltpu.VMEM((LEN, HD), BF16),
    gcols=pltpu.VMEM((TEMB, HD), BF16),
    emb=pltpu.VMEM((8, TEMB), F32),
    embs=pltpu.VMEM((16, 8, TEMB), F32),
    rows_send=pltpu.VMEM((256, ZD + 128), BF16),
    rows_got=pltpu.VMEM((256, ZD + 128), BF16),
    liftf=pltpu.VMEM((4, 4, 128, PH), BF16),
    outf=pltpu.VMEM((4, 4, 64, ZD), BF16),
    o32=pltpu.VMEM((LEN, HD), F32),
    lse=pltpu.VMEM((8, LEN), F32),
    gated=pltpu.VMEM((LEN, HD), BF16),
    mix_tok=pltpu.VMEM((TOK, FEAT), BF16),
    hid2=pltpu.VMEM((2 * TOK, FEAT), BF16),
    act2=pltpu.VMEM((2 * TOK, PH), BF16),
    gpf=pltpu.VMEM((2, TOK, ZD // 2), BF16),
    gp2=pltpu.VMEM((2 * TOK, ZD // 2), BF16),
    glf=pltpu.VMEM((2, TOK, PH // 2), BF16),
    gl2=pltpu.VMEM((2 * TOK, PH // 2), BF16),
    ghs=pltpu.VMEM((TOK, FEAT), BF16),
    gh=pltpu.VMEM((LEN, HD), BF16),
    do=pltpu.VMEM((LEN, HD), BF16),
    drow=pltpu.VMEM((8, LEN), F32),
    dq32=pltpu.VMEM((LEN, HD), F32),
    dqb=pltpu.VMEM((LEN, HD), BF16),
    dkb=pltpu.VMEM((LEN, HD), BF16),
    dvb=pltpu.VMEM((LEN, HD), BF16),
    ggs=pltpu.VMEM((8, HD), F32),
    ggall=pltpu.VMEM((16, 8, HD), F32),
    gfull=pltpu.VMEM((TEMB, HD), F32),
    gsl=pltpu.VMEM((16, HD), F32),
    gl_x=pltpu.VMEM((4, 4, 128, PH // 2), BF16),
    go_x=pltpu.VMEM((4, 4, 64, ZD // 2), BF16),
    rl_x=pltpu.VMEM((3, 4, 128, PH // 2), BF16),
    ro_y=pltpu.VMEM((3, 4, 4, 16, ZD // 2), BF16),
    gl_y=pltpu.VMEM((4, 128, PH // 2), BF16),
    go_y=pltpu.VMEM((4, 4, 16, ZD // 2), BF16),
    rl_y=pltpu.VMEM((3, 4, 32, PH // 2), BF16),
    ro_x=pltpu.VMEM((3, 4, 16, ZD // 2), BF16),
    gl_z=pltpu.VMEM((4, 32, PH // 2), BF16),
    go_z=pltpu.VMEM((4, 16, ZD // 2), BF16),
    rl_z=pltpu.VMEM((3, 32, PH // 2), BF16),
    ro_z=pltpu.VMEM((3, 16, ZD // 2), BF16),
    hl_z=pltpu.VMEM((2, 32, PH // 2), BF16),
    ho_z=pltpu.VMEM((2, 16, ZD // 2), BF16),
    pl_f=pltpu.VMEM((32, PH // 2), BF16),
    po_f=pltpu.VMEM((16, ZD // 2), BF16),
    lift_sum=pltpu.VMEM((128, PH), BF16),
    out_sum=pltpu.VMEM((64, ZD), BF16),
    s_a2a=pltpu.SemaphoreType.DMA((8, 16)),
    r_a2a=pltpu.SemaphoreType.DMA((8, 16)),
    s_rel=pltpu.SemaphoreType.DMA((16,)),
    r_rel=pltpu.SemaphoreType.DMA((16,)),
    s_gate=pltpu.SemaphoreType.DMA((4, 16)),
    r_gate=pltpu.SemaphoreType.DMA((4, 16)),
    s_w=pltpu.SemaphoreType.DMA((2, 13)),
    r_w=pltpu.SemaphoreType.DMA((2, 13)),
    s_pair=pltpu.SemaphoreType.DMA((4,)),
    r_pair=pltpu.SemaphoreType.DMA((4,)),
    s_red=pltpu.SemaphoreType.DMA((2, 20)),
    r_red=pltpu.SemaphoreType.DMA((2, 20)),
    local=pltpu.SemaphoreType.DMA((20,)),
)
NAMES = list(SCRATCH)


def dot(a, b, dims, precision=None):
    return lax.dot_general(
        a, b, (dims, ((), ())), precision=precision, preferred_element_type=F32
    )


def step_kernel(*refs):
    q, k, v, res, enc, gain, bias, trow, when, gate, lift, outw = refs[:12]
    dq, dk, dv, ggate, glift, gout = refs[12:18]
    s = dict(zip(NAMES, refs[18:]))
    dp, me = lax.axis_index("dp"), lax.axis_index("seq")
    zl, x = lax.div(dp, 4), lax.rem(dp, 4)
    zh, yc = lax.div(me, 8), lax.rem(me, 8)
    y, c = lax.div(yc, 2), lax.rem(yc, 2)
    z = zh * 4 + zl
    partner = (dp, me + 1 - 2 * c)

    def at_x(i):
        return (zl * 4 + lax.rem(x + i, 4), me)

    def at_y(i):
        return (dp, zh * 8 + lax.rem(y + i, 4) * 2 + c)

    def at_z(i):
        to = lax.rem(z + i, 8)
        return (lax.rem(to, 4) * 4 + x, lax.div(to, 4) * 8 + yc)

    def at_yc(i):
        return (dp, zh * 8 + lax.rem(yc + i, 8))

    def cols(j):
        return pl.ds(pl.multiple_of(j * 128, 128), 128)

    def remote(src, dst, send, recv, device):
        return pltpu.make_async_remote_copy(
            src_ref=src, dst_ref=dst, send_sem=send, recv_sem=recv,
            device_id=device, device_id_type=MESH,
        )

    finish = []

    def go(*copy):
        made = remote(*copy)
        made.start()
        finish.append(made.wait_send)
        return made

    half = TEMB // 2
    index = lax.broadcasted_iota(jnp.int32, (8, half), 1).astype(F32)
    angles = when[0].astype(F32) * jnp.exp(-math.log(10000.0) * index / half)
    s["emb"][:, :half] = jnp.cos(angles).astype(BF16).astype(F32)
    s["emb"][:, half:] = jnp.sin(angles).astype(BF16).astype(F32)

    barrier = pltpu.get_barrier_semaphore()

    def greet(i, _):
        pl.semaphore_signal(barrier, 1, device_id=(dp, lax.rem(me + i, 16)), device_id_type=MESH)
        pl.semaphore_signal(barrier, 1, device_id=(lax.rem(dp + i, 16), me), device_id_type=MESH)
        return 0

    lax.fori_loop(1, 16, greet, 0)
    for i in range(1, 4):
        other = (lax.rem(zl + i, 4) * 4 + x, (1 - zh) * 8 + yc)
        pl.semaphore_signal(barrier, 1, device_id=other, device_id_type=MESH)
    pl.semaphore_wait(barrier, 33)

    def tok_to_head(t, src, dst):
        def copy(j, owner):
            return remote(
                src.at[:, cols(j)], dst.at[cols(owner), :],
                s["s_a2a"].at[t, j], s["r_a2a"].at[t, owner], (dp, j),
            )

        def start(i, _):
            copy(lax.rem(me + i, 16), me).start()
            return 0

        own = pltpu.make_async_copy(src.at[:, cols(me)], dst.at[cols(me), :], s["local"].at[t])
        own.start()
        lax.fori_loop(1, 16, start, 0)

        def wait():
            def one(i, _):
                j = lax.rem(me + i, 16)
                copy(j, j).wait_recv()
                return 0

            own.wait()
            lax.fori_loop(1, 16, one, 0)

        def sent():
            def one(i, _):
                copy(lax.rem(me + i, 16), me).wait_send()
                return 0

            lax.fori_loop(1, 16, one, 0)

        finish.append(sent)
        return wait

    def head_to_tok(t, src, dst):
        def copy(j, owner):
            return remote(
                src.at[cols(j), :], dst.at[:, cols(owner)],
                s["s_a2a"].at[t, j], s["r_a2a"].at[t, owner], (dp, j),
            )

        own = pltpu.make_async_copy(src.at[cols(me), :], dst.at[:, cols(me)], s["local"].at[t])

        def send(j):
            @pl.when(j != me)
            def _():
                copy(j, me).start()

            @pl.when(j == me)
            def _():
                own.start()

        def wait():
            def one(i, _):
                j = lax.rem(me + i, 16)
                copy(j, j).wait_recv()
                return 0

            own.wait()
            lax.fori_loop(1, 16, one, 0)

        def sent():
            def one(i, _):
                copy(lax.rem(me + i, 16), me).wait_send()
                return 0

            lax.fori_loop(1, 16, one, 0)

        finish.append(sent)
        return send, wait

    def spread(t, src_of, dst_of, index, device_of):
        def copy(j, owner):
            return remote(
                src_of(j), dst_of(owner), s["s_gate"].at[t, j], s["r_gate"].at[t, owner],
                device_of(j),
            )

        def start(i, _):
            copy(lax.rem(index + i, 16), index).start()
            return 0

        own = pltpu.make_async_copy(src_of(index), dst_of(index), s["local"].at[8 + t])
        own.start()
        lax.fori_loop(1, 16, start, 0)

        def wait():
            def one(i, _):
                j = lax.rem(index + i, 16)
                copy(j, j).wait_recv()
                return 0

            own.wait()
            lax.fori_loop(1, 16, one, 0)

        def sent():
            def one(i, _):
                copy(lax.rem(index + i, 16), index).wait_send()
                return 0

            lax.fori_loop(1, 16, one, 0)

        finish.append(sent)
        return wait

    weights = [(lift, s["liftf"], 64, 256), (outw, s["outf"], 32, 384)]
    z_hops = [at_z(1), at_z(7), at_z(2 + 4 * c)]
    along_z = []
    for n, (shard, full, height, width) in enumerate(weights):
        rows = pl.ds(pl.multiple_of(c * height, height), height)
        part = pl.ds(pl.multiple_of(y * width, 128), width)
        for i, device in enumerate(z_hops):
            along_z.append(
                go(shard.at[rows, part], full.at[zl, x, rows, part],
                   s["s_w"].at[n, i], s["r_w"].at[n, i], device).wait_recv
            )
        own = pltpu.make_async_copy(
            shard.at[rows, part], full.at[zl, x, rows, part], s["local"].at[12 + n]
        )
        own.start()
        along_z.append(own.wait)
    got_q = tok_to_head(0, q, s["qh"])
    got_k = tok_to_head(1, k, s["kh"])
    got_v = tok_to_head(2, v, s["vh"])
    got_gate = spread(
        0, lambda j: gate.at[:, cols(me)],
        lambda j: s["gcols"].at[pl.ds(pl.multiple_of(j * 16, 16), 16), :], dp,
        lambda j: (j, me),
    )
    got_emb = spread(1, lambda j: s["emb"], lambda j: s["embs"].at[j], dp, lambda j: (j, me))

    wide = enc[...].astype(F32)
    centred = wide - jnp.mean(wide, axis=-1, keepdims=True)
    variance = jnp.mean(centred * centred, axis=-1, keepdims=True)
    normed = (centred * lax.rsqrt(variance + EPSILON) * gain[...][None] + bias[...][None]).astype(BF16)
    tcol = jnp.transpose(jnp.broadcast_to(trow[...], (TOK, TOK)))
    own_row, own_col = lax.shift_right_logical(trow[...], 7), lax.shift_right_logical(tcol, 7)
    before = lax.broadcasted_iota(jnp.int32, (TOK, TOK), 0) < lax.broadcasted_iota(
        jnp.int32, (TOK, TOK), 1
    )
    same = jnp.where((own_col == own_row) & before, 1.0, 0.0)
    slot = own_row.astype(F32) * 16.0 + jnp.sum(same, axis=0, keepdims=True)
    place = ((tcol & 127) + 1).astype(F32).astype(BF16)
    slots = lax.broadcasted_iota(jnp.int32, (256, TOK), 0).astype(F32)
    pick = jnp.where(slots == slot, 1.0, 0.0).astype(BF16)
    s["rows_send"][:, :ZD] = dot(pick, normed, ((1,), (0,))).astype(BF16)
    s["rows_send"][:, ZD:] = dot(pick, place, ((1,), (0,))).astype(BF16)

    def relay(j, owner):
        return remote(
            s["rows_send"].at[pl.ds(pl.multiple_of(j * 16, 16), 16), :],
            s["rows_got"].at[pl.ds(pl.multiple_of(owner * 16, 16), 16), :],
            s["s_rel"].at[j], s["r_rel"].at[owner], (dp, j),
        )

    def relay_start(i, _):
        relay(lax.rem(me + i, 16), me).start()
        return 0

    def relay_sent():
        def one(i, _):
            relay(lax.rem(me + i, 16), me).wait_send()
            return 0

        lax.fori_loop(1, 16, one, 0)

    finish.append(relay_sent)

    for wait in along_z:
        wait()
    def second(n, i, piece, device):
        return go(piece, piece, s["s_w"].at[n, i], s["r_w"].at[n, i], device)

    lift_rows = pl.ds(pl.multiple_of(c * 64, 64), 64)
    out_rows = pl.ds(pl.multiple_of(c * 32, 32), 32)

    def lift_cols(at):
        return pl.ds(pl.multiple_of(lax.rem(at, 4) * 256, 128), 256)

    def out_cols(at):
        return pl.ds(pl.multiple_of(lax.rem(at, 4) * 384, 128), 384)

    lift_y = [
        second(0, 2 + i, s["liftf"].at[:, x, lift_rows, lift_cols(y)], at_y(i))
        for i in range(1, 4)
    ]
    out_x = [
        second(1, 2 + i, s["outf"].at[:, x, out_rows, out_cols(y)], at_x(i))
        for i in range(1, 4)
    ]

    def lift_to_core(i):
        return second(0, 9 + i, s["liftf"].at[:, lax.rem(x + 4 - i, 4), lift_rows, :], partner)

    def out_to_core(i):
        return second(1, 9 + i, s["outf"].at[:, :, out_rows, out_cols(y + 4 - i)], partner)

    for copy in lift_y:
        copy.wait_recv()
    lift_x = [
        second(0, 5 + i, s["liftf"].at[:, x, lift_rows, :], at_x(i)) for i in range(1, 4)
    ]
    for copy in out_x:
        copy.wait_recv()
    out_y = [
        second(1, 5 + i, s["outf"].at[:, :, out_rows, out_cols(y)], at_y(i)) for i in range(1, 4)
    ]
    lift_core, out_core = [lift_to_core(0)], [out_to_core(0)]

    got_gate()
    gating = dot(s["emb"][...].astype(BF16), s["gcols"][...], ((1,), (0,)))[0:1]
    got_q()
    got_k()
    got_v()
    lax.fori_loop(1, 16, relay_start, 0)
    mine = pl.ds(pl.multiple_of(me * 16, 16), 16)
    relay_own = pltpu.make_async_copy(
        s["rows_send"].at[mine, :], s["rows_got"].at[mine, :], s["local"].at[14]
    )
    relay_own.start()

    send_mix, got_mix = head_to_tok(3, s["gated"], s["mix_tok"])

    def forward(i, _):
        block = lax.rem(lax.div(me, 2) + i, LEN // QB)
        at = pl.ds(pl.multiple_of(block * QB, QB), QB)
        scores = dot(s["qh"][at, :], s["kh"][...], ((1,), (1,)))
        most = jnp.max(scores, axis=1, keepdims=True)
        shifted = jnp.exp2((scores - most) * LOG2)
        weight = jnp.sum(shifted, axis=1, keepdims=True)
        mixed = dot(shifted.astype(BF16), s["vh"][...], ((1,), (0,))) / weight
        s["o32"][at, :] = mixed
        s["gated"][at, :] = (gating * mixed.astype(BF16).astype(F32)).astype(BF16)
        level = jnp.broadcast_to(most * LOG2 + jnp.log2(weight), (QB, 128))
        s["lse"][:, at] = jnp.transpose(level)[0:8]
        send_mix(2 * block)
        send_mix(2 * block + 1)
        return 0

    lax.fori_loop(0, LEN // QB, forward, 0)
    for i, copy in enumerate(lift_x):
        copy.wait_recv()
        lift_core.append(lift_to_core(i + 1))
    for i, copy in enumerate(out_y):
        copy.wait_recv()
        out_core.append(out_to_core(i + 1))

    def relay_wait(i, _):
        j = lax.rem(me + i, 16)
        relay(j, j).wait_recv()
        return 0

    relay_own.wait()
    lax.fori_loop(1, 16, relay_wait, 0)
    tokens = lax.broadcasted_iota(jnp.int32, (256, TOK), 1).astype(F32) + 1.0
    placed = jnp.where(s["rows_got"][:, ZD : ZD + 1].astype(F32) == tokens, 1.0, 0.0).astype(BF16)
    target = dot(placed, s["rows_got"][:, :ZD], ((0,), (0,)))
    target_norm = jnp.sqrt(jnp.sum(target * target, axis=1, keepdims=True) + EPSILON)

    got_mix()
    hidden = (res[...].astype(F32) + s["mix_tok"][...].astype(F32)).astype(BF16)
    s["hid2"][0:TOK, :] = hidden
    pair = [
        go(s["hid2"].at[0:TOK, :], s["hid2"].at[TOK:, :],
           s["s_pair"].at[0], s["r_pair"].at[0], partner)
    ]
    for copy in lift_core:
        copy.wait_recv()
    lifted = jnp.zeros((TOK, PH), F32)
    for i in range(4):
        lifted += dot(
            s["hid2"][0:TOK, i * 512 : (i + 1) * 512],
            s["liftf"][i].reshape(512, PH), ((1,), (0,)),
        )
    sigmoid = jax.nn.sigmoid(lifted)
    s["act2"][0:TOK, :] = (lifted * sigmoid).astype(BF16)
    slope = sigmoid * (1.0 + lifted * (1.0 - sigmoid))
    pair.append(
        go(s["act2"].at[0:TOK, :], s["act2"].at[TOK:, :],
           s["s_pair"].at[1], s["r_pair"].at[1], partner)
    )
    for copy in out_core:
        copy.wait_recv()
    predicted = jnp.zeros((TOK, ZD), F32)
    for i in range(4):
        predicted += dot(
            s["act2"][0:TOK, i * 256 : (i + 1) * 256],
            s["outf"][i].reshape(256, ZD), ((1,), (0,)),
        )
    pred_norm = jnp.sqrt(jnp.sum(predicted * predicted, axis=1, keepdims=True) + EPSILON)
    both = pred_norm * target_norm
    cosine = jnp.sum(predicted * target, axis=1, keepdims=True) / both
    grad_pred = (
        (-1.0 * ZD) * (target / both - cosine * predicted / (pred_norm * pred_norm))
    ).astype(BF16)
    s["gpf"][0] = grad_pred[:, : ZD // 2]
    s["gpf"][1] = grad_pred[:, ZD // 2 :]
    pair.append(
        go(s["gpf"].at[1 - c], s["gp2"].at[TOK:, :], s["s_pair"].at[2], s["r_pair"].at[2], partner)
    )
    for i in range(4):
        at = slice(i * 256, (i + 1) * 256)
        grad_act = dot(grad_pred, s["outf"][i].reshape(256, ZD), ((1,), (1,)))
        s["glf"][i // 2, :, (i % 2) * 256 : (i % 2 + 1) * 256] = (
            grad_act * slope[:, at]
        ).astype(BF16)
    pair.append(
        go(s["glf"].at[1 - c], s["gl2"].at[TOK:, :], s["s_pair"].at[3], s["r_pair"].at[3], partner)
    )
    grad_lifted = jnp.concatenate([s["glf"][0], s["glf"][1]], axis=1)
    for i in range(4):
        s["ghs"][:, i * 512 : (i + 1) * 512] = dot(
            grad_lifted, s["liftf"][i].reshape(512, PH), ((1,), (1,))
        ).astype(BF16)
    got_grad = tok_to_head(4, s["ghs"], s["gh"])

    s["gp2"][0:TOK, :] = s["gpf"][c]
    s["gl2"][0:TOK, :] = s["glf"][c]
    for copy in pair:
        copy.wait_recv()

    def lift_part(i, _):
        s["gl_x"][lax.div(i, 4), lax.rem(i, 4)] = dot(
            s["hid2"][:, cols(i)], s["gl2"][...], ((0,), (0,))
        ).astype(BF16)
        return 0

    lax.fori_loop(0, 16, lift_part, 0)

    def out_part(i, _):
        done = dot(s["act2"][:, cols(i)], s["gp2"][...], ((0,), (0,))).astype(BF16)
        first = 2 * i
        s["go_x"][lax.div(first, 4), lax.rem(first, 4)] = done[:64]
        s["go_x"][lax.div(first, 4), lax.rem(first, 4) + 1] = done[64:]
        return 0

    lax.fori_loop(0, 8, out_part, 0)
    sums = []
    for i in range(1, 4):
        rows = pl.ds(pl.multiple_of(lax.rem(y + i, 4) * 16, 16), 16)
        sums.append(
            go(s["gl_x"].at[:, lax.rem(x + i, 4)], s["rl_x"].at[i - 1],
               s["s_red"].at[0, i - 1], s["r_red"].at[0, i - 1], at_x(i))
        )
        sums.append(
            go(s["go_x"].at[:, :, rows, :], s["ro_y"].at[i - 1],
               s["s_red"].at[1, i - 1], s["r_red"].at[1, i - 1], at_y(i))
        )

    def total(own, room):
        added = own.astype(F32)
        for i in range(room.shape[0]):
            added += room[i].astype(F32)
        return added

    got_grad()
    ones = jnp.ones((8, HD), F32)

    def prepare(i, partial):
        at = pl.ds(pl.multiple_of(i * QB, QB), QB)
        grad = s["gh"][at, :].astype(F32)
        mixed = s["o32"][at, :]
        scaled = (gating * grad).astype(BF16)
        s["do"][at, :] = scaled
        s["drow"][:, at] = dot(
            ones, scaled.astype(F32) * mixed, ((1,), (1,)), lax.Precision.HIGHEST
        )
        product = grad * mixed.astype(BF16).astype(F32)
        return partial + jnp.sum(product.reshape(QB // 8, 8, HD), axis=0)

    s["ggs"][...] = lax.fori_loop(0, LEN // QB, prepare, jnp.zeros((8, HD), F32))
    got_gg = spread(2, lambda j: s["ggs"], lambda j: s["ggall"].at[j], dp, lambda j: (j, me))
    s["dq32"][...] = jnp.zeros((LEN, HD), F32)
    send_dk, got_dk = head_to_tok(5, s["dkb"], dk)
    send_dv, got_dv = head_to_tok(6, s["dvb"], dv)
    send_dq, got_dq = head_to_tok(7, s["dqb"], dq)

    def backward(i, _):
        block = lax.rem(lax.div(me, 2) + i, LEN // KB)
        at = pl.ds(pl.multiple_of(block * KB, KB), KB)
        keys = s["kh"][at, :]
        scores = dot(keys, s["qh"][...], ((1,), (1,)))
        chances = jnp.exp2(scores * LOG2 - s["lse"][0:1, :])
        s["dvb"][at, :] = dot(chances.astype(BF16), s["do"][...], ((1,), (0,))).astype(BF16)
        grad_chances = dot(s["vh"][at, :], s["do"][...], ((1,), (1,)))
        grad_scores = (chances * (grad_chances - s["drow"][0:1, :])).astype(BF16)
        s["dkb"][at, :] = (dot(grad_scores, s["qh"][...], ((1,), (0,))) * SCALE).astype(BF16)
        for send in (send_dv, send_dk):
            send(2 * block)
            send(2 * block + 1)
        s["dq32"][...] += dot(grad_scores, keys, ((0,), (0,)))
        return 0

    lax.fori_loop(0, EARLY, backward, 0)

    for copy in sums:
        copy.wait_recv()
    s["gl_y"][...] = total(s["gl_x"][:, x], s["rl_x"]).astype(BF16)
    y_rows = pl.ds(pl.multiple_of(y * 16, 16), 16)
    s["go_y"][...] = total(s["go_x"][:, :, y_rows, :], s["ro_y"]).astype(BF16)
    sums = []
    for i in range(1, 4):
        rows = pl.ds(pl.multiple_of(lax.rem(y + i, 4) * 32, 32), 32)
        sums.append(
            go(s["gl_y"].at[:, rows, :], s["rl_y"].at[i - 1],
               s["s_red"].at[0, 2 + i], s["r_red"].at[0, 2 + i], at_y(i))
        )
        sums.append(
            go(s["go_y"].at[:, lax.rem(x + i, 4)], s["ro_x"].at[i - 1],
               s["s_red"].at[1, 2 + i], s["r_red"].at[1, 2 + i], at_x(i))
        )
    lax.fori_loop(EARLY, LEN // KB, backward, 0)
    s["dqb"][...] = (s["dq32"][...] * SCALE).astype(BF16)

    def send_queries(i, _):
        send_dq(lax.rem(me + i, 16))
        return 0

    lax.fori_loop(0, 16, send_queries, 0)

    for copy in sums:
        copy.wait_recv()
    y_rows = pl.ds(pl.multiple_of(y * 32, 32), 32)
    s["gl_z"][...] = total(s["gl_y"][:, y_rows, :], s["rl_y"]).astype(BF16)
    s["go_z"][...] = total(s["go_y"][:, x], s["ro_x"]).astype(BF16)
    sums = []
    for n, (part, room) in enumerate([("gl_z", "rl_z"), ("go_z", "ro_z")]):
        for i, hop in enumerate((1, 7, 2 + 4 * c)):
            sums.append(
                go(s[part].at[lax.rem(z + hop, 4)], s[room].at[i],
                   s["s_red"].at[n, 6 + i], s["r_red"].at[n, 6 + i], at_z(hop))
            )

    got_emb()
    got_gg()
    s["gfull"][...] = dot(
        s["embs"][...].reshape(128, TEMB), s["ggall"][...].reshape(128, HD), ((0,), (0,)),
        lax.Precision.HIGHEST,
    )
    s["gsl"][...] = s["gfull"][pl.ds(pl.multiple_of(dp * 16, 16), 16), :]
    got_ggate = spread(
        3, lambda j: s["gsl"], lambda j: ggate.at[:, cols(j)], me, lambda j: (dp, j)
    )

    for copy in sums:
        copy.wait_recv()
    sums = []
    halves = [("gl_z", "rl_z", "hl_z"), ("go_z", "ro_z", "ho_z")]
    for n, (part, room, side) in enumerate(halves):
        s[side][0] = total(s[part][zl], s[room]).astype(BF16)
        sums.append(
            go(s[side].at[0], s[side].at[1], s["s_red"].at[n, 9], s["r_red"].at[n, 9], at_z(4))
        )
    for copy in sums:
        copy.wait_recv()
    sums = []
    final = [
        ("hl_z", "pl_f", "lift_sum", 32, PH // 2),
        ("ho_z", "po_f", "out_sum", 16, ZD // 2),
    ]
    for n, (side, piece, whole, height, width) in enumerate(final):
        added = (s[side][0].astype(F32) + s[side][1].astype(F32)).astype(BF16)
        s[piece][...] = added
        rows = pl.ds(pl.multiple_of(y * height, height), height)
        part = pl.ds(pl.multiple_of(c * width, 128), width)
        s[whole][rows, part] = added
        for i in range(1, 8):
            sums.append(
                go(s[piece], s[whole].at[rows, part],
                   s["s_red"].at[n, 12 + i], s["r_red"].at[n, 12 + i], at_yc(i))
            )
    got_ggate()
    for copy in sums:
        copy.wait_recv()
    for whole, out, n in (("lift_sum", glift, 15), ("out_sum", gout, 16)):
        own = pltpu.make_async_copy(s[whole], out, s["local"].at[n])
        own.start()
        finish.append(own.wait)
    got_dk()
    got_dv()
    got_dq()
    for wait in finish:
        wait()


def copy_kernel(*refs):
    for i in range(6):
        refs[6 + i][...] = refs[i][...].astype(refs[6 + i].dtype)


def shards(
    queries,
    key_states,
    value_states,
    residual,
    enc_hidden,
    enc_gain,
    enc_bias,
    feature_target,
    timestep,
    gate_weight,
    lift_weight,
    out_weight,
):
    anywhere = pl.BlockSpec(memory_space=pl.ANY)
    near = pl.BlockSpec(memory_space=pltpu.VMEM)
    tok = jax.ShapeDtypeStruct((TOK, FEAT), BF16)
    out_shape = (
        tok, tok, tok,
        jax.ShapeDtypeStruct((16, FEAT), F32),
        jax.ShapeDtypeStruct((128, PH), F32),
        jax.ShapeDtypeStruct((64, ZD), F32),
    )
    outs = pl.pallas_call(
        step_kernel,
        out_shape=out_shape[:4]
        + (jax.ShapeDtypeStruct((128, PH), BF16), jax.ShapeDtypeStruct((64, ZD), BF16)),
        in_specs=[anywhere] * 3 + [near] * 5 + [pl.BlockSpec(memory_space=pltpu.SMEM)]
        + [anywhere] * 3,
        out_specs=(anywhere,) * 6,
        scratch_shapes=list(SCRATCH.values()),
        compiler_params=pltpu.CompilerParams(
            collective_id=0, has_side_effects=True, vmem_limit_bytes=60 << 20
        ),
        name="repa_step",
    )(
        queries[0], key_states[0], value_states[0], residual[0], enc_hidden[0],
        enc_gain, enc_bias, feature_target, timestep, gate_weight, lift_weight, out_weight,
    )
    d_queries, d_keys, d_values, grad_gate, grad_lift, grad_out = pl.pallas_call(
        copy_kernel,
        out_shape=out_shape,
        grid=(2,),
        in_specs=[pl.BlockSpec((a.shape[0] // 2, a.shape[1]), lambda i: (i, 0)) for a in out_shape],
        out_specs=[pl.BlockSpec((a.shape[0] // 2, a.shape[1]), lambda i: (i, 0)) for a in out_shape],
        compiler_params=pltpu.CompilerParams(vmem_limit_bytes=32 << 20),
        name="hand_out",
    )(*outs)
    return (d_queries[None], d_keys[None], d_values[None], grad_gate, grad_lift, grad_out)


def solution(mesh):
    tokens = P("dp", "seq", None)
    rows = P("dp", None)
    in_specs = (tokens,) * 5 + (P(), P(), P("dp", "seq"), P("dp"), rows, rows, rows)
    out_specs = (tokens,) * 3 + (rows,) * 3
    return jax.shard_map(
        shards, mesh=mesh, in_specs=in_specs, out_specs=out_specs, check_vma=False
    )
```

```python
import functools
import math

import jax
import jax.numpy as jnp
from jax import lax
from jax.experimental import pallas as pl
from jax.experimental.pallas import tpu as pltpu
from jax.sharding import PartitionSpec as P

HD = 128
ZD = 1536
PH = 1024
FEAT = 2048
TEMB = 256
LEN = 2048
TOK = 128
EPSILON = 1e-06
SCALE = HD ** (-0.5)
LOG2 = SCALE * math.log2(math.e)
QB = 256
KB = 256
EARLY = 6
MESH = pl.DeviceIdType.MESH
F32 = jnp.float32
BF16 = jnp.bfloat16

SCRATCH = dict(
    qh=pltpu.VMEM((LEN, HD), BF16),
    kh=pltpu.VMEM((LEN, HD), BF16),
    vh=pltpu.VMEM((LEN, HD), BF16),
    gcols=pltpu.VMEM((TEMB, HD), BF16),
    emb=pltpu.VMEM((8, TEMB), F32),
    embs=pltpu.VMEM((16, 8, TEMB), F32),
    rows_send=pltpu.VMEM((256, ZD + 128), BF16),
    rows_got=pltpu.VMEM((256, ZD + 128), BF16),
    liftf=pltpu.VMEM((4, 4, 128, PH), BF16),
    outf=pltpu.VMEM((4, 4, 64, ZD), BF16),
    o32=pltpu.VMEM((LEN, HD), F32),
    lse=pltpu.VMEM((8, LEN), F32),
    gated=pltpu.VMEM((LEN, HD), BF16),
    mix_tok=pltpu.VMEM((TOK, FEAT), BF16),
    hid2=pltpu.VMEM((2 * TOK, FEAT), BF16),
    act2=pltpu.VMEM((2 * TOK, PH), BF16),
    gpf=pltpu.VMEM((2, TOK, ZD // 2), BF16),
    gp2=pltpu.VMEM((2 * TOK, ZD // 2), BF16),
    glf=pltpu.VMEM((2, TOK, PH // 2), BF16),
    gl2=pltpu.VMEM((2 * TOK, PH // 2), BF16),
    ghs=pltpu.VMEM((TOK, FEAT), BF16),
    gh=pltpu.VMEM((LEN, HD), BF16),
    do=pltpu.VMEM((LEN, HD), BF16),
    drow=pltpu.VMEM((8, LEN), F32),
    dq32=pltpu.VMEM((LEN, HD), F32),
    dqb=pltpu.VMEM((LEN, HD), BF16),
    dkb=pltpu.VMEM((LEN, HD), BF16),
    dvb=pltpu.VMEM((LEN, HD), BF16),
    ggs=pltpu.VMEM((8, HD), F32),
    ggall=pltpu.VMEM((16, 8, HD), F32),
    gfull=pltpu.VMEM((TEMB, HD), F32),
    gsl=pltpu.VMEM((16, HD), F32),
    gl_x=pltpu.VMEM((4, 4, 128, PH // 2), BF16),
    go_x=pltpu.VMEM((4, 4, 64, ZD // 2), BF16),
    rl_x=pltpu.VMEM((3, 4, 128, PH // 2), BF16),
    ro_y=pltpu.VMEM((3, 4, 4, 16, ZD // 2), BF16),
    gl_y=pltpu.VMEM((4, 128, PH // 2), BF16),
    go_y=pltpu.VMEM((4, 4, 16, ZD // 2), BF16),
    rl_y=pltpu.VMEM((3, 4, 32, PH // 2), BF16),
    ro_x=pltpu.VMEM((3, 4, 16, ZD // 2), BF16),
    gl_z=pltpu.VMEM((4, 32, PH // 2), BF16),
    go_z=pltpu.VMEM((4, 16, ZD // 2), BF16),
    rl_z=pltpu.VMEM((3, 32, PH // 2), BF16),
    ro_z=pltpu.VMEM((3, 16, ZD // 2), BF16),
    hl_z=pltpu.VMEM((2, 32, PH // 2), BF16),
    ho_z=pltpu.VMEM((2, 16, ZD // 2), BF16),
    pl_f=pltpu.VMEM((32, PH // 2), BF16),
    po_f=pltpu.VMEM((16, ZD // 2), BF16),
    lift_sum=pltpu.VMEM((128, PH), BF16),
    out_sum=pltpu.VMEM((64, ZD), BF16),
    s_a2a=pltpu.SemaphoreType.DMA((8, 16)),
    r_a2a=pltpu.SemaphoreType.DMA((8, 16)),
    s_rel=pltpu.SemaphoreType.DMA((16,)),
    r_rel=pltpu.SemaphoreType.DMA((16,)),
    s_gate=pltpu.SemaphoreType.DMA((4, 16)),
    r_gate=pltpu.SemaphoreType.DMA((4, 16)),
    s_w=pltpu.SemaphoreType.DMA((2, 13)),
    r_w=pltpu.SemaphoreType.DMA((2, 13)),
    s_pair=pltpu.SemaphoreType.DMA((4,)),
    r_pair=pltpu.SemaphoreType.DMA((4,)),
    s_red=pltpu.SemaphoreType.DMA((2, 20)),
    r_red=pltpu.SemaphoreType.DMA((2, 20)),
    local=pltpu.SemaphoreType.DMA((20,)),
)
NAMES = list(SCRATCH)


def dot(a, b, dims, precision=None):
    return lax.dot_general(
        a, b, (dims, ((), ())), precision=precision, preferred_element_type=F32
    )


def step_kernel(*refs):
    q, k, v, res, enc, gain, bias, trow, when, gate, lift, outw = refs[:12]
    dq, dk, dv, ggate, glift, gout = refs[12:18]
    s = dict(zip(NAMES, refs[18:]))
    dp, me = lax.axis_index("dp"), lax.axis_index("seq")
    zl, x = lax.div(dp, 4), lax.rem(dp, 4)
    zh, yc = lax.div(me, 8), lax.rem(me, 8)
    y, c = lax.div(yc, 2), lax.rem(yc, 2)
    z = zh * 4 + zl
    partner = (dp, me + 1 - 2 * c)

    def at_x(i):
        return (zl * 4 + lax.rem(x + i, 4), me)

    def at_y(i):
        return (dp, zh * 8 + lax.rem(y + i, 4) * 2 + c)

    def at_z(i):
        to = lax.rem(z + i, 8)
        return (lax.rem(to, 4) * 4 + x, lax.div(to, 4) * 8 + yc)

    def at_yc(i):
        return (dp, zh * 8 + lax.rem(yc + i, 8))

    def cols(j):
        return pl.ds(pl.multiple_of(j * 128, 128), 128)

    def remote(src, dst, send, recv, device):
        return pltpu.make_async_remote_copy(
            src_ref=src, dst_ref=dst, send_sem=send, recv_sem=recv,
            device_id=device, device_id_type=MESH,
        )

    finish = []

    def go(*copy):
        made = remote(*copy)
        made.start()
        finish.append(made.wait_send)
        return made

    half = TEMB // 2
    index = lax.broadcasted_iota(jnp.int32, (8, half), 1).astype(F32)
    angles = when[0].astype(F32) * jnp.exp(-math.log(10000.0) * index / half)
    s["emb"][:, :half] = jnp.cos(angles).astype(BF16).astype(F32)
    s["emb"][:, half:] = jnp.sin(angles).astype(BF16).astype(F32)

    barrier = pltpu.get_barrier_semaphore()

    def greet(i, _):
        pl.semaphore_signal(barrier, 1, device_id=(dp, lax.rem(me + i, 16)), device_id_type=MESH)
        pl.semaphore_signal(barrier, 1, device_id=(lax.rem(dp + i, 16), me), device_id_type=MESH)
        return 0

    lax.fori_loop(1, 16, greet, 0)
    for i in range(1, 4):
        other = (lax.rem(zl + i, 4) * 4 + x, (1 - zh) * 8 + yc)
        pl.semaphore_signal(barrier, 1, device_id=other, device_id_type=MESH)
    pl.semaphore_wait(barrier, 33)

    def tok_to_head(t, src, dst):
        def copy(j, owner):
            return remote(
                src.at[:, cols(j)], dst.at[cols(owner), :],
                s["s_a2a"].at[t, j], s["r_a2a"].at[t, owner], (dp, j),
            )

        def far(i, _):
            copy((1 - zh) * 8 + lax.rem(yc + i, 8), me).start()
            return 0

        def near(i, _):
            copy(zh * 8 + lax.rem(yc + i, 8), me).start()
            return 0

        own = pltpu.make_async_copy(src.at[:, cols(me)], dst.at[cols(me), :], s["local"].at[t])

        def start_far():
            lax.fori_loop(0, 8, far, 0)

        def start_near():
            own.start()
            lax.fori_loop(1, 8, near, 0)

        def wait():
            def one(i, _):
                j = lax.rem(me + i, 16)
                copy(j, j).wait_recv()
                return 0

            own.wait()
            lax.fori_loop(1, 16, one, 0)

        def sent():
            def one(i, _):
                copy(lax.rem(me + i, 16), me).wait_send()
                return 0

            lax.fori_loop(1, 16, one, 0)

        finish.append(sent)
        return start_far, start_near, wait

    def head_to_tok(t, src, dst):
        def copy(j, owner):
            return remote(
                src.at[cols(j), :], dst.at[:, cols(owner)],
                s["s_a2a"].at[t, j], s["r_a2a"].at[t, owner], (dp, j),
            )

        own = pltpu.make_async_copy(src.at[cols(me), :], dst.at[:, cols(me)], s["local"].at[t])

        def send(j):
            @pl.when(j != me)
            def _():
                copy(j, me).start()

            @pl.when(j == me)
            def _():
                own.start()

        def wait():
            def one(i, _):
                j = lax.rem(me + i, 16)
                copy(j, j).wait_recv()
                return 0

            own.wait()
            lax.fori_loop(1, 16, one, 0)

        def sent():
            def one(i, _):
                copy(lax.rem(me + i, 16), me).wait_send()
                return 0

            lax.fori_loop(1, 16, one, 0)

        finish.append(sent)
        return send, wait

    def spread(t, src_of, dst_of, index, device_of):
        def copy(j, owner):
            return remote(
                src_of(j), dst_of(owner), s["s_gate"].at[t, j], s["r_gate"].at[t, owner],
                device_of(j),
            )

        def start(i, _):
            copy(lax.rem(index + i, 16), index).start()
            return 0

        own = pltpu.make_async_copy(src_of(index), dst_of(index), s["local"].at[8 + t])
        own.start()
        lax.fori_loop(1, 16, start, 0)

        def wait():
            def one(i, _):
                j = lax.rem(index + i, 16)
                copy(j, j).wait_recv()
                return 0

            own.wait()
            lax.fori_loop(1, 16, one, 0)

        def sent():
            def one(i, _):
                copy(lax.rem(index + i, 16), index).wait_send()
                return 0

            lax.fori_loop(1, 16, one, 0)

        finish.append(sent)
        return wait

    weights = [(lift, s["liftf"], 64, 256), (outw, s["outf"], 32, 384)]
    z_hops = [at_z(1), at_z(7), at_z(2 + 4 * c)]
    along_z = []
    for n, (shard, full, height, width) in enumerate(weights):
        rows = pl.ds(pl.multiple_of(c * height, height), height)
        part = pl.ds(pl.multiple_of(y * width, 128), width)
        for i, device in enumerate(z_hops):
            along_z.append(
                go(shard.at[rows, part], full.at[zl, x, rows, part],
                   s["s_w"].at[n, i], s["r_w"].at[n, i], device).wait_recv
            )
        own = pltpu.make_async_copy(
            shard.at[rows, part], full.at[zl, x, rows, part], s["local"].at[12 + n]
        )
        own.start()
        along_z.append(own.wait)
    far_q, near_q, got_q = tok_to_head(0, q, s["qh"])
    far_k, near_k, got_k = tok_to_head(1, k, s["kh"])
    far_v, near_v, got_v = tok_to_head(2, v, s["vh"])
    for start in (far_q, far_k, far_v, near_q, near_k, near_v):
        start()
    got_gate = spread(
        0, lambda j: gate.at[:, cols(me)],
        lambda j: s["gcols"].at[pl.ds(pl.multiple_of(j * 16, 16), 16), :], dp,
        lambda j: (j, me),
    )
    got_emb = spread(1, lambda j: s["emb"], lambda j: s["embs"].at[j], dp, lambda j: (j, me))

    wide = enc[...].astype(F32)
    centred = wide - jnp.mean(wide, axis=-1, keepdims=True)
    variance = jnp.mean(centred * centred, axis=-1, keepdims=True)
    normed = (centred * lax.rsqrt(variance + EPSILON) * gain[...][None] + bias[...][None]).astype(BF16)
    tcol = jnp.transpose(jnp.broadcast_to(trow[...], (TOK, TOK)))
    own_row, own_col = lax.shift_right_logical(trow[...], 7), lax.shift_right_logical(tcol, 7)
    before = lax.broadcasted_iota(jnp.int32, (TOK, TOK), 0) < lax.broadcasted_iota(
        jnp.int32, (TOK, TOK), 1
    )
    same = jnp.where((own_col == own_row) & before, 1.0, 0.0)
    slot = own_row.astype(F32) * 16.0 + jnp.sum(same, axis=0, keepdims=True)
    place = ((tcol & 127) + 1).astype(F32).astype(BF16)
    slots = lax.broadcasted_iota(jnp.int32, (256, TOK), 0).astype(F32)
    pick = jnp.where(slots == slot, 1.0, 0.0).astype(BF16)
    s["rows_send"][:, :ZD] = dot(pick, normed, ((1,), (0,))).astype(BF16)
    s["rows_send"][:, ZD:] = dot(pick, place, ((1,), (0,))).astype(BF16)

    def relay(j, owner):
        return remote(
            s["rows_send"].at[pl.ds(pl.multiple_of(j * 16, 16), 16), :],
            s["rows_got"].at[pl.ds(pl.multiple_of(owner * 16, 16), 16), :],
            s["s_rel"].at[j], s["r_rel"].at[owner], (dp, j),
        )

    def relay_near(i, _):
        relay(zh * 8 + lax.rem(yc + i, 8), me).start()
        return 0

    def relay_far(i, _):
        relay((1 - zh) * 8 + lax.rem(yc + i, 8), me).start()
        return 0

    def relay_sent():
        def one(i, _):
            relay(lax.rem(me + i, 16), me).wait_send()
            return 0

        lax.fori_loop(1, 16, one, 0)

    finish.append(relay_sent)

    for wait in along_z:
        wait()
    def second(n, i, piece, device):
        return go(piece, piece, s["s_w"].at[n, i], s["r_w"].at[n, i], device)

    lift_rows = pl.ds(pl.multiple_of(c * 64, 64), 64)
    out_rows = pl.ds(pl.multiple_of(c * 32, 32), 32)

    def lift_cols(at):
        return pl.ds(pl.multiple_of(lax.rem(at, 4) * 256, 128), 256)

    def out_cols(at):
        return pl.ds(pl.multiple_of(lax.rem(at, 4) * 384, 128), 384)

    lift_y = [
        second(0, 2 + i, s["liftf"].at[:, x, lift_rows, lift_cols(y)], at_y(i))
        for i in range(1, 4)
    ]
    out_x = [
        second(1, 2 + i, s["outf"].at[:, x, out_rows, out_cols(y)], at_x(i))
        for i in range(1, 4)
    ]

    def lift_to_core(i):
        return second(0, 9 + i, s["liftf"].at[:, lax.rem(x + 4 - i, 4), lift_rows, :], partner)

    def out_to_core(i):
        return second(1, 9 + i, s["outf"].at[:, :, out_rows, out_cols(y + 4 - i)], partner)

    for copy in lift_y:
        copy.wait_recv()
    lift_x = [
        second(0, 5 + i, s["liftf"].at[:, x, lift_rows, :], at_x(i)) for i in range(1, 4)
    ]
    for copy in out_x:
        copy.wait_recv()
    out_y = [
        second(1, 5 + i, s["outf"].at[:, :, out_rows, out_cols(y)], at_y(i)) for i in range(1, 4)
    ]
    lift_core, out_core = [lift_to_core(0)], [out_to_core(0)]

    got_gate()
    gating = dot(s["emb"][...].astype(BF16), s["gcols"][...], ((1,), (0,)))[0:1]
    got_q()
    got_k()
    got_v()
    lax.fori_loop(1, 8, relay_near, 0)
    mine = pl.ds(pl.multiple_of(me * 16, 16), 16)
    relay_own = pltpu.make_async_copy(
        s["rows_send"].at[mine, :], s["rows_got"].at[mine, :], s["local"].at[14]
    )
    relay_own.start()

    send_mix, got_mix = head_to_tok(3, s["gated"], s["mix_tok"])

    def forward(i, _):
        block = lax.rem(lax.div(me, 2) + i, LEN // QB)
        at = pl.ds(pl.multiple_of(block * QB, QB), QB)
        scores = dot(s["qh"][at, :], s["kh"][...], ((1,), (1,)))
        most = jnp.max(scores, axis=1, keepdims=True)
        shifted = jnp.exp2((scores - most) * LOG2)
        weight = jnp.sum(shifted, axis=1, keepdims=True)
        mixed = dot(shifted.astype(BF16), s["vh"][...], ((1,), (0,))) / weight
        s["o32"][at, :] = mixed
        s["gated"][at, :] = (gating * mixed.astype(BF16).astype(F32)).astype(BF16)
        level = jnp.broadcast_to(most * LOG2 + jnp.log2(weight), (QB, 128))
        s["lse"][:, at] = jnp.transpose(level)[0:8]
        send_mix(2 * block)
        send_mix(2 * block + 1)
        return 0

    lax.fori_loop(0, LEN // QB, forward, 0)
    lax.fori_loop(0, 8, relay_far, 0)
    for i, copy in enumerate(lift_x):
        copy.wait_recv()
        lift_core.append(lift_to_core(i + 1))
    for i, copy in enumerate(out_y):
        copy.wait_recv()
        out_core.append(out_to_core(i + 1))

    got_mix()
    hidden = (res[...].astype(F32) + s["mix_tok"][...].astype(F32)).astype(BF16)
    s["hid2"][0:TOK, :] = hidden
    pair = [
        go(s["hid2"].at[0:TOK, :], s["hid2"].at[TOK:, :],
           s["s_pair"].at[0], s["r_pair"].at[0], partner)
    ]
    for copy in lift_core:
        copy.wait_recv()
    lifted = jnp.zeros((TOK, PH), F32)
    for i in range(4):
        lifted += dot(
            s["hid2"][0:TOK, i * 512 : (i + 1) * 512],
            s["liftf"][i].reshape(512, PH), ((1,), (0,)),
        )
    sigmoid = jax.nn.sigmoid(lifted)
    s["act2"][0:TOK, :] = (lifted * sigmoid).astype(BF16)
    slope = sigmoid * (1.0 + lifted * (1.0 - sigmoid))
    pair.append(
        go(s["act2"].at[0:TOK, :], s["act2"].at[TOK:, :],
           s["s_pair"].at[1], s["r_pair"].at[1], partner)
    )
    for copy in out_core:
        copy.wait_recv()
    predicted = jnp.zeros((TOK, ZD), F32)
    for i in range(4):
        predicted += dot(
            s["act2"][0:TOK, i * 256 : (i + 1) * 256],
            s["outf"][i].reshape(256, ZD), ((1,), (0,)),
        )
    def relay_wait(i, _):
        j = lax.rem(me + i, 16)
        relay(j, j).wait_recv()
        return 0

    relay_own.wait()
    lax.fori_loop(1, 16, relay_wait, 0)
    tokens = lax.broadcasted_iota(jnp.int32, (256, TOK), 1).astype(F32) + 1.0
    placed = jnp.where(s["rows_got"][:, ZD : ZD + 1].astype(F32) == tokens, 1.0, 0.0).astype(BF16)
    target = dot(placed, s["rows_got"][:, :ZD], ((0,), (0,)))
    target_norm = jnp.sqrt(jnp.sum(target * target, axis=1, keepdims=True) + EPSILON)

    pred_norm = jnp.sqrt(jnp.sum(predicted * predicted, axis=1, keepdims=True) + EPSILON)
    both = pred_norm * target_norm
    cosine = jnp.sum(predicted * target, axis=1, keepdims=True) / both
    grad_pred = (
        (-1.0 * ZD) * (target / both - cosine * predicted / (pred_norm * pred_norm))
    ).astype(BF16)
    s["gpf"][0] = grad_pred[:, : ZD // 2]
    s["gpf"][1] = grad_pred[:, ZD // 2 :]
    pair.append(
        go(s["gpf"].at[1 - c], s["gp2"].at[TOK:, :], s["s_pair"].at[2], s["r_pair"].at[2], partner)
    )
    for i in range(4):
        at = slice(i * 256, (i + 1) * 256)
        grad_act = dot(grad_pred, s["outf"][i].reshape(256, ZD), ((1,), (1,)))
        s["glf"][i // 2, :, (i % 2) * 256 : (i % 2 + 1) * 256] = (
            grad_act * slope[:, at]
        ).astype(BF16)
    pair.append(
        go(s["glf"].at[1 - c], s["gl2"].at[TOK:, :], s["s_pair"].at[3], s["r_pair"].at[3], partner)
    )
    grad_lifted = jnp.concatenate([s["glf"][0], s["glf"][1]], axis=1)
    for i in range(4):
        s["ghs"][:, i * 512 : (i + 1) * 512] = dot(
            grad_lifted, s["liftf"][i].reshape(512, PH), ((1,), (1,))
        ).astype(BF16)
    far_grad, near_grad, got_grad = tok_to_head(4, s["ghs"], s["gh"])
    far_grad()
    near_grad()

    s["gp2"][0:TOK, :] = s["gpf"][c]
    s["gl2"][0:TOK, :] = s["glf"][c]
    for copy in pair:
        copy.wait_recv()

    def lift_part(i, _):
        s["gl_x"][lax.div(i, 4), lax.rem(i, 4)] = dot(
            s["hid2"][:, cols(i)], s["gl2"][...], ((0,), (0,))
        ).astype(BF16)
        return 0

    lax.fori_loop(0, 16, lift_part, 0)

    def out_part(i, _):
        done = dot(s["act2"][:, cols(i)], s["gp2"][...], ((0,), (0,))).astype(BF16)
        first = 2 * i
        s["go_x"][lax.div(first, 4), lax.rem(first, 4)] = done[:64]
        s["go_x"][lax.div(first, 4), lax.rem(first, 4) + 1] = done[64:]
        return 0

    lax.fori_loop(0, 8, out_part, 0)
    sums = []
    for i in range(1, 4):
        rows = pl.ds(pl.multiple_of(lax.rem(y + i, 4) * 16, 16), 16)
        sums.append(
            go(s["gl_x"].at[:, lax.rem(x + i, 4)], s["rl_x"].at[i - 1],
               s["s_red"].at[0, i - 1], s["r_red"].at[0, i - 1], at_x(i))
        )
        sums.append(
            go(s["go_x"].at[:, :, rows, :], s["ro_y"].at[i - 1],
               s["s_red"].at[1, i - 1], s["r_red"].at[1, i - 1], at_y(i))
        )

    def total(own, room):
        added = own.astype(F32)
        for i in range(room.shape[0]):
            added += room[i].astype(F32)
        return added

    got_grad()
    ones = jnp.ones((8, HD), BF16)

    def prepare(i, partial):
        at = pl.ds(pl.multiple_of(i * QB, QB), QB)
        grad = s["gh"][at, :].astype(F32)
        mixed = s["o32"][at, :]
        scaled = (gating * grad).astype(BF16)
        s["do"][at, :] = scaled
        inner = scaled.astype(F32) * mixed
        upper = inner.astype(BF16)
        lower = (inner - upper.astype(F32)).astype(BF16)
        s["drow"][:, at] = dot(ones, upper, ((1,), (1,))) + dot(ones, lower, ((1,), (1,)))
        product = grad * mixed.astype(BF16).astype(F32)
        return partial + jnp.sum(product.reshape(QB // 8, 8, HD), axis=0)

    s["ggs"][...] = lax.fori_loop(0, LEN // QB, prepare, jnp.zeros((8, HD), F32))
    got_gg = spread(2, lambda j: s["ggs"], lambda j: s["ggall"].at[j], dp, lambda j: (j, me))
    s["dq32"][...] = jnp.zeros((LEN, HD), F32)
    send_dk, got_dk = head_to_tok(5, s["dkb"], dk)
    send_dv, got_dv = head_to_tok(6, s["dvb"], dv)
    send_dq, got_dq = head_to_tok(7, s["dqb"], dq)

    def backward(i, _):
        block = lax.rem(lax.div(me, 2) + i, LEN // KB)
        at = pl.ds(pl.multiple_of(block * KB, KB), KB)
        keys = s["kh"][at, :]
        scores = dot(keys, s["qh"][...], ((1,), (1,)))
        chances = jnp.exp2(scores * LOG2 - s["lse"][0:1, :])
        s["dvb"][at, :] = dot(chances.astype(BF16), s["do"][...], ((1,), (0,))).astype(BF16)
        grad_chances = dot(s["vh"][at, :], s["do"][...], ((1,), (1,)))
        grad_scores = (chances * (grad_chances - s["drow"][0:1, :])).astype(BF16)
        s["dkb"][at, :] = (dot(grad_scores, s["qh"][...], ((1,), (0,))) * SCALE).astype(BF16)
        for send in (send_dv, send_dk):
            send(2 * block)
            send(2 * block + 1)
        s["dq32"][...] += dot(grad_scores, keys, ((0,), (0,)))
        return 0

    lax.fori_loop(0, EARLY, backward, 0)

    for copy in sums:
        copy.wait_recv()
    s["gl_y"][...] = total(s["gl_x"][:, x], s["rl_x"]).astype(BF16)
    y_rows = pl.ds(pl.multiple_of(y * 16, 16), 16)
    s["go_y"][...] = total(s["go_x"][:, :, y_rows, :], s["ro_y"]).astype(BF16)
    sums = []
    for i in range(1, 4):
        rows = pl.ds(pl.multiple_of(lax.rem(y + i, 4) * 32, 32), 32)
        sums.append(
            go(s["gl_y"].at[:, rows, :], s["rl_y"].at[i - 1],
               s["s_red"].at[0, 2 + i], s["r_red"].at[0, 2 + i], at_y(i))
        )
        sums.append(
            go(s["go_y"].at[:, lax.rem(x + i, 4)], s["ro_x"].at[i - 1],
               s["s_red"].at[1, 2 + i], s["r_red"].at[1, 2 + i], at_x(i))
        )
    lax.fori_loop(EARLY, LEN // KB, backward, 0)
    for copy in sums:
        copy.wait_recv()
    y_rows = pl.ds(pl.multiple_of(y * 32, 32), 32)
    s["gl_z"][...] = total(s["gl_y"][:, y_rows, :], s["rl_y"]).astype(BF16)
    s["go_z"][...] = total(s["go_y"][:, x], s["ro_x"]).astype(BF16)
    sums = []
    for n, (part, room) in enumerate([("gl_z", "rl_z"), ("go_z", "ro_z")]):
        for i, hop in enumerate((1, 7, 2 + 4 * c)):
            sums.append(
                go(s[part].at[lax.rem(z + hop, 4)], s[room].at[i],
                   s["s_red"].at[n, 6 + i], s["r_red"].at[n, 6 + i], at_z(hop))
            )

    s["dqb"][...] = (s["dq32"][...] * SCALE).astype(BF16)

    def send_queries(i, _):
        half = lax.rem(1 - zh + lax.div(i, 8), 2)
        send_dq(half * 8 + lax.rem(yc + i, 8))
        return 0

    lax.fori_loop(0, 16, send_queries, 0)

    got_emb()
    got_gg()
    s["gfull"][...] = dot(
        s["embs"][...].reshape(128, TEMB), s["ggall"][...].reshape(128, HD), ((0,), (0,)),
        lax.Precision.HIGHEST,
    )
    s["gsl"][...] = s["gfull"][pl.ds(pl.multiple_of(dp * 16, 16), 16), :]
    got_ggate = spread(
        3, lambda j: s["gsl"], lambda j: ggate.at[:, cols(j)], me, lambda j: (dp, j)
    )

    for copy in sums:
        copy.wait_recv()
    sums = []
    halves = [("gl_z", "rl_z", "hl_z"), ("go_z", "ro_z", "ho_z")]
    for n, (part, room, side) in enumerate(halves):
        s[side][0] = total(s[part][zl], s[room]).astype(BF16)
        sums.append(
            go(s[side].at[0], s[side].at[1], s["s_red"].at[n, 9], s["r_red"].at[n, 9], at_z(4))
        )
    for copy in sums:
        copy.wait_recv()
    sums = []
    final = [
        ("hl_z", "pl_f", "lift_sum", 32, PH // 2),
        ("ho_z", "po_f", "out_sum", 16, ZD // 2),
    ]
    for n, (side, piece, whole, height, width) in enumerate(final):
        added = (s[side][0].astype(F32) + s[side][1].astype(F32)).astype(BF16)
        s[piece][...] = added
        rows = pl.ds(pl.multiple_of(y * height, height), height)
        part = pl.ds(pl.multiple_of(c * width, 128), width)
        s[whole][rows, part] = added
        for i in range(1, 8):
            sums.append(
                go(s[piece], s[whole].at[rows, part],
                   s["s_red"].at[n, 12 + i], s["r_red"].at[n, 12 + i], at_yc(i))
            )
    got_ggate()
    for copy in sums:
        copy.wait_recv()
    for whole, out, n in (("lift_sum", glift, 15), ("out_sum", gout, 16)):
        own = pltpu.make_async_copy(s[whole], out, s["local"].at[n])
        own.start()
        finish.append(own.wait)
    got_dk()
    got_dv()
    got_dq()
    for wait in finish:
        wait()


def copy_kernel(*refs):
    for i in range(6):
        refs[6 + i][...] = refs[i][...].astype(refs[6 + i].dtype)


def shards(
    queries,
    key_states,
    value_states,
    residual,
    enc_hidden,
    enc_gain,
    enc_bias,
    feature_target,
    timestep,
    gate_weight,
    lift_weight,
    out_weight,
):
    anywhere = pl.BlockSpec(memory_space=pl.ANY)
    near = pl.BlockSpec(memory_space=pltpu.VMEM)
    tok = jax.ShapeDtypeStruct((TOK, FEAT), BF16)
    out_shape = (
        tok, tok, tok,
        jax.ShapeDtypeStruct((16, FEAT), F32),
        jax.ShapeDtypeStruct((128, PH), F32),
        jax.ShapeDtypeStruct((64, ZD), F32),
    )
    outs = pl.pallas_call(
        step_kernel,
        out_shape=out_shape[:4]
        + (jax.ShapeDtypeStruct((128, PH), BF16), jax.ShapeDtypeStruct((64, ZD), BF16)),
        in_specs=[anywhere] * 3 + [near] * 5 + [pl.BlockSpec(memory_space=pltpu.SMEM)]
        + [anywhere] * 3,
        out_specs=(anywhere,) * 6,
        scratch_shapes=list(SCRATCH.values()),
        compiler_params=pltpu.CompilerParams(
            collective_id=0, has_side_effects=True, vmem_limit_bytes=60 << 20
        ),
        name="repa_step",
    )(
        queries[0], key_states[0], value_states[0], residual[0], enc_hidden[0],
        enc_gain, enc_bias, feature_target, timestep, gate_weight, lift_weight, out_weight,
    )
    d_queries, d_keys, d_values, grad_gate, grad_lift, grad_out = pl.pallas_call(
        copy_kernel,
        out_shape=out_shape,
        grid=(2,),
        in_specs=[pl.BlockSpec((a.shape[0] // 2, a.shape[1]), lambda i: (i, 0)) for a in out_shape],
        out_specs=[pl.BlockSpec((a.shape[0] // 2, a.shape[1]), lambda i: (i, 0)) for a in out_shape],
        compiler_params=pltpu.CompilerParams(vmem_limit_bytes=60 << 20),
        name="hand_out",
    )(*outs)
    return (d_queries[None], d_keys[None], d_values[None], grad_gate, grad_lift, grad_out)


def solution(mesh):
    tokens = P("dp", "seq", None)
    rows = P("dp", None)
    in_specs = (tokens,) * 5 + (P(), P(), P("dp", "seq"), P("dp"), rows, rows, rows)
    out_specs = (tokens,) * 3 + (rows,) * 3
    return jax.shard_map(
        shards, mesh=mesh, in_specs=in_specs, out_specs=out_specs, check_vma=False
    )
```

```python
import functools
import math

import jax
import jax.numpy as jnp
from jax import lax
from jax.experimental import pallas as pl
from jax.experimental.pallas import tpu as pltpu
from jax.sharding import PartitionSpec as P

HD = 128
ZD = 1536
PH = 1024
FEAT = 2048
TEMB = 256
LEN = 2048
TOK = 128
EPSILON = 1e-06
SCALE = HD ** (-0.5)
LOG2 = SCALE * math.log2(math.e)
QB = 256
KB = 256
EARLY = 6
MESH = pl.DeviceIdType.MESH
F32 = jnp.float32
BF16 = jnp.bfloat16

SCRATCH = dict(
    qh=pltpu.VMEM((LEN, HD), BF16),
    kh=pltpu.VMEM((LEN, HD), BF16),
    vh=pltpu.VMEM((LEN, HD), BF16),
    gcols=pltpu.VMEM((TEMB, HD), BF16),
    emb=pltpu.VMEM((8, TEMB), F32),
    embs=pltpu.VMEM((16, 8, TEMB), F32),
    rows_send=pltpu.VMEM((256, ZD + 128), BF16),
    rows_got=pltpu.VMEM((256, ZD + 128), BF16),
    liftf=pltpu.VMEM((4, 4, 128, PH), BF16),
    outf=pltpu.VMEM((4, 4, 64, ZD), BF16),
    o32=pltpu.VMEM((LEN, HD), F32),
    lse=pltpu.VMEM((8, LEN), F32),
    gated=pltpu.VMEM((LEN, HD), BF16),
    mix_tok=pltpu.VMEM((TOK, FEAT), BF16),
    hid2=pltpu.VMEM((2 * TOK, FEAT), BF16),
    act2=pltpu.VMEM((2 * TOK, PH), BF16),
    gpf=pltpu.VMEM((2, TOK, ZD // 2), BF16),
    gp2=pltpu.VMEM((2 * TOK, ZD // 2), BF16),
    glf=pltpu.VMEM((2, TOK, PH // 2), BF16),
    gl2=pltpu.VMEM((2 * TOK, PH // 2), BF16),
    glw=pltpu.VMEM((TOK, PH), BF16),
    ghs=pltpu.VMEM((TOK, FEAT), BF16),
    gh=pltpu.VMEM((LEN, HD), BF16),
    do=pltpu.VMEM((LEN, HD), BF16),
    drow=pltpu.VMEM((8, LEN), F32),
    dq32=pltpu.VMEM((LEN, HD), F32),
    dqb=pltpu.VMEM((LEN, HD), BF16),
    dkb=pltpu.VMEM((LEN, HD), BF16),
    dvb=pltpu.VMEM((LEN, HD), BF16),
    ggs=pltpu.VMEM((8, HD), F32),
    ggall=pltpu.VMEM((16, 8, HD), F32),
    gfull=pltpu.VMEM((TEMB, HD), F32),
    gsl=pltpu.VMEM((16, HD), F32),
    gl_x=pltpu.VMEM((4, 4, 128, PH // 2), BF16),
    go_x=pltpu.VMEM((4, 4, 64, ZD // 2), BF16),
    rl_x=pltpu.VMEM((3, 4, 128, PH // 2), BF16),
    ro_y=pltpu.VMEM((3, 4, 4, 16, ZD // 2), BF16),
    gl_y=pltpu.VMEM((4, 128, PH // 2), BF16),
    go_y=pltpu.VMEM((4, 4, 16, ZD // 2), BF16),
    rl_y=pltpu.VMEM((3, 4, 32, PH // 2), BF16),
    ro_x=pltpu.VMEM((3, 4, 16, ZD // 2), BF16),
    gl_z=pltpu.VMEM((4, 32, PH // 2), BF16),
    go_z=pltpu.VMEM((4, 16, ZD // 2), BF16),
    rl_z=pltpu.VMEM((3, 32, PH // 2), BF16),
    ro_z=pltpu.VMEM((3, 16, ZD // 2), BF16),
    hl_z=pltpu.VMEM((2, 32, PH // 2), BF16),
    ho_z=pltpu.VMEM((2, 16, ZD // 2), BF16),
    pl_f=pltpu.VMEM((32, PH // 2), BF16),
    po_f=pltpu.VMEM((16, ZD // 2), BF16),
    lift_sum=pltpu.VMEM((128, PH), BF16),
    out_sum=pltpu.VMEM((64, ZD), BF16),
    s_a2a=pltpu.SemaphoreType.DMA((8, 16)),
    r_a2a=pltpu.SemaphoreType.DMA((8, 16)),
    s_rel=pltpu.SemaphoreType.DMA((16,)),
    r_rel=pltpu.SemaphoreType.DMA((16,)),
    s_gate=pltpu.SemaphoreType.DMA((4, 16)),
    r_gate=pltpu.SemaphoreType.DMA((4, 16)),
    s_w=pltpu.SemaphoreType.DMA((2, 13)),
    r_w=pltpu.SemaphoreType.DMA((2, 13)),
    s_pair=pltpu.SemaphoreType.DMA((4,)),
    r_pair=pltpu.SemaphoreType.DMA((4,)),
    s_red=pltpu.SemaphoreType.DMA((2, 20)),
    r_red=pltpu.SemaphoreType.DMA((2, 20)),
    local=pltpu.SemaphoreType.DMA((20,)),
)
NAMES = list(SCRATCH)


def dot(a, b, dims, precision=None):
    return lax.dot_general(
        a, b, (dims, ((), ())), precision=precision, preferred_element_type=F32
    )


def step_kernel(*refs):
    q, k, v, res, enc, gain, bias, trow, when, gate, lift, outw = refs[:12]
    dq, dk, dv, ggate, glift, gout = refs[12:18]
    s = dict(zip(NAMES, refs[18:]))
    dp, me = lax.axis_index("dp"), lax.axis_index("seq")
    zl, x = lax.div(dp, 4), lax.rem(dp, 4)
    zh, yc = lax.div(me, 8), lax.rem(me, 8)
    y, c = lax.div(yc, 2), lax.rem(yc, 2)
    z = zh * 4 + zl
    partner = (dp, me + 1 - 2 * c)

    def at_x(i):
        return (zl * 4 + lax.rem(x + i, 4), me)

    def at_y(i):
        return (dp, zh * 8 + lax.rem(y + i, 4) * 2 + c)

    def at_z(i):
        to = lax.rem(z + i, 8)
        return (lax.rem(to, 4) * 4 + x, lax.div(to, 4) * 8 + yc)

    def at_yc(i):
        return (dp, zh * 8 + lax.rem(yc + i, 8))

    def cols(j):
        return pl.ds(pl.multiple_of(j * 128, 128), 128)

    def remote(src, dst, send, recv, device):
        return pltpu.make_async_remote_copy(
            src_ref=src, dst_ref=dst, send_sem=send, recv_sem=recv,
            device_id=device, device_id_type=MESH,
        )

    finish = []

    def go(*copy):
        made = remote(*copy)
        made.start()
        finish.append(made.wait_send)
        return made

    half = TEMB // 2
    index = lax.broadcasted_iota(jnp.int32, (8, half), 1).astype(F32)
    angles = when[0].astype(F32) * jnp.exp(-math.log(10000.0) * index / half)
    s["emb"][:, :half] = jnp.cos(angles).astype(BF16).astype(F32)
    s["emb"][:, half:] = jnp.sin(angles).astype(BF16).astype(F32)

    barrier = pltpu.get_barrier_semaphore()

    def greet(i, _):
        pl.semaphore_signal(barrier, 1, device_id=(dp, lax.rem(me + i, 16)), device_id_type=MESH)
        pl.semaphore_signal(barrier, 1, device_id=(lax.rem(dp + i, 16), me), device_id_type=MESH)
        return 0

    lax.fori_loop(1, 16, greet, 0)
    for i in range(1, 4):
        other = (lax.rem(zl + i, 4) * 4 + x, (1 - zh) * 8 + yc)
        pl.semaphore_signal(barrier, 1, device_id=other, device_id_type=MESH)
    pl.semaphore_wait(barrier, 33)

    def tok_to_head(t, src, dst):
        def copy(j, owner):
            return remote(
                src.at[:, cols(j)], dst.at[cols(owner), :],
                s["s_a2a"].at[t, j], s["r_a2a"].at[t, owner], (dp, j),
            )

        def far(i, _):
            copy(lax.rem(me + i + 8, 16), me).start()
            return 0

        def near(i, _):
            copy(lax.rem(me + i, 16), me).start()
            return 0

        own = pltpu.make_async_copy(src.at[:, cols(me)], dst.at[cols(me), :], s["local"].at[t])

        def send(j):
            @pl.when(j != me)
            def _():
                copy(j, me).start()

            @pl.when(j == me)
            def _():
                own.start()

        def start_far():
            lax.fori_loop(0, 8, far, 0)

        def start_near():
            own.start()
            lax.fori_loop(1, 8, near, 0)

        def wait():
            def one(i, _):
                j = lax.rem(me + i, 16)
                copy(j, j).wait_recv()
                return 0

            own.wait()
            lax.fori_loop(1, 16, one, 0)

        def sent():
            def one(i, _):
                copy(lax.rem(me + i, 16), me).wait_send()
                return 0

            lax.fori_loop(1, 16, one, 0)

        finish.append(sent)
        return start_far, start_near, send, wait

    def head_to_tok(t, src, dst):
        def copy(j, owner):
            return remote(
                src.at[cols(j), :], dst.at[:, cols(owner)],
                s["s_a2a"].at[t, j], s["r_a2a"].at[t, owner], (dp, j),
            )

        own = pltpu.make_async_copy(src.at[cols(me), :], dst.at[:, cols(me)], s["local"].at[t])

        def send(j):
            @pl.when(j != me)
            def _():
                copy(j, me).start()

            @pl.when(j == me)
            def _():
                own.start()

        def wait():
            def one(i, _):
                j = lax.rem(me + i, 16)
                copy(j, j).wait_recv()
                return 0

            own.wait()
            lax.fori_loop(1, 16, one, 0)

        def sent():
            def one(i, _):
                copy(lax.rem(me + i, 16), me).wait_send()
                return 0

            lax.fori_loop(1, 16, one, 0)

        finish.append(sent)
        return send, wait

    def spread(t, src_of, dst_of, index, device_of):
        def copy(j, owner):
            return remote(
                src_of(j), dst_of(owner), s["s_gate"].at[t, j], s["r_gate"].at[t, owner],
                device_of(j),
            )

        def start(i, _):
            copy(lax.rem(index + i, 16), index).start()
            return 0

        own = pltpu.make_async_copy(src_of(index), dst_of(index), s["local"].at[8 + t])
        own.start()
        lax.fori_loop(1, 16, start, 0)

        def wait():
            def one(i, _):
                j = lax.rem(index + i, 16)
                copy(j, j).wait_recv()
                return 0

            own.wait()
            lax.fori_loop(1, 16, one, 0)

        def sent():
            def one(i, _):
                copy(lax.rem(index + i, 16), index).wait_send()
                return 0

            lax.fori_loop(1, 16, one, 0)

        finish.append(sent)
        return wait

    weights = [(lift, s["liftf"], 64, 256), (outw, s["outf"], 32, 384)]
    z_hops = [at_z(1), at_z(7), at_z(2 + 4 * c)]
    along_z = []
    for n, (shard, full, height, width) in enumerate(weights):
        rows = pl.ds(pl.multiple_of(c * height, height), height)
        part = pl.ds(pl.multiple_of(y * width, 128), width)
        for i, device in enumerate(z_hops):
            along_z.append(
                go(shard.at[rows, part], full.at[zl, x, rows, part],
                   s["s_w"].at[n, i], s["r_w"].at[n, i], device).wait_recv
            )
        own = pltpu.make_async_copy(
            shard.at[rows, part], full.at[zl, x, rows, part], s["local"].at[12 + n]
        )
        own.start()
        along_z.append(own.wait)
    far_q, near_q, _, got_q = tok_to_head(0, q, s["qh"])
    far_k, near_k, _, got_k = tok_to_head(1, k, s["kh"])
    far_v, near_v, _, got_v = tok_to_head(2, v, s["vh"])
    for start in (near_q, far_q, near_k, far_k, near_v, far_v):
        start()
    got_gate = spread(
        0, lambda j: gate.at[:, cols(me)],
        lambda j: s["gcols"].at[pl.ds(pl.multiple_of(j * 16, 16), 16), :], dp,
        lambda j: (j, me),
    )
    got_emb = spread(1, lambda j: s["emb"], lambda j: s["embs"].at[j], dp, lambda j: (j, me))

    wide = enc[...].astype(F32)
    centred = wide - jnp.mean(wide, axis=-1, keepdims=True)
    variance = jnp.mean(centred * centred, axis=-1, keepdims=True)
    normed = (centred * lax.rsqrt(variance + EPSILON) * gain[...][None] + bias[...][None]).astype(BF16)
    tcol = jnp.transpose(jnp.broadcast_to(trow[...], (TOK, TOK)))
    own_row, own_col = lax.shift_right_logical(trow[...], 7), lax.shift_right_logical(tcol, 7)
    before = lax.broadcasted_iota(jnp.int32, (TOK, TOK), 0) < lax.broadcasted_iota(
        jnp.int32, (TOK, TOK), 1
    )
    same = jnp.where((own_col == own_row) & before, 1.0, 0.0)
    slot = own_row.astype(F32) * 16.0 + jnp.sum(same, axis=0, keepdims=True)
    place = ((tcol & 127) + 1).astype(F32).astype(BF16)
    slots = lax.broadcasted_iota(jnp.int32, (256, TOK), 0).astype(F32)
    pick = jnp.where(slots == slot, 1.0, 0.0).astype(BF16)
    s["rows_send"][:, :ZD] = dot(pick, normed, ((1,), (0,))).astype(BF16)
    s["rows_send"][:, ZD:] = dot(pick, place, ((1,), (0,))).astype(BF16)

    def relay(j, owner):
        return remote(
            s["rows_send"].at[pl.ds(pl.multiple_of(j * 16, 16), 16), :],
            s["rows_got"].at[pl.ds(pl.multiple_of(owner * 16, 16), 16), :],
            s["s_rel"].at[j], s["r_rel"].at[owner], (dp, j),
        )

    def relay_near(i, _):
        relay(zh * 8 + lax.rem(yc + i, 8), me).start()
        return 0

    def relay_far(i, _):
        relay((1 - zh) * 8 + lax.rem(yc + i, 8), me).start()
        return 0

    def relay_sent():
        def one(i, _):
            relay(lax.rem(me + i, 16), me).wait_send()
            return 0

        lax.fori_loop(1, 16, one, 0)

    finish.append(relay_sent)

    lax.fori_loop(1, 8, relay_near, 0)
    lax.fori_loop(0, 8, relay_far, 0)
    mine = pl.ds(pl.multiple_of(me * 16, 16), 16)
    relay_own = pltpu.make_async_copy(
        s["rows_send"].at[mine, :], s["rows_got"].at[mine, :], s["local"].at[14]
    )
    relay_own.start()

    for wait in along_z:
        wait()
    def second(n, i, piece, device):
        return go(piece, piece, s["s_w"].at[n, i], s["r_w"].at[n, i], device)

    lift_rows = pl.ds(pl.multiple_of(c * 64, 64), 64)
    out_rows = pl.ds(pl.multiple_of(c * 32, 32), 32)

    def lift_cols(at):
        return pl.ds(pl.multiple_of(lax.rem(at, 4) * 256, 128), 256)

    def out_cols(at):
        return pl.ds(pl.multiple_of(lax.rem(at, 4) * 384, 128), 384)

    lift_y = [
        second(0, 2 + i, s["liftf"].at[:, x, lift_rows, lift_cols(y)], at_y(i))
        for i in range(1, 4)
    ]
    out_x = [
        second(1, 2 + i, s["outf"].at[:, x, out_rows, out_cols(y)], at_x(i))
        for i in range(1, 4)
    ]

    def lift_to_core(i):
        return second(0, 9 + i, s["liftf"].at[:, lax.rem(x + 4 - i, 4), lift_rows, :], partner)

    def out_to_core(i):
        return second(1, 9 + i, s["outf"].at[:, :, out_rows, out_cols(y + 4 - i)], partner)

    for copy in lift_y:
        copy.wait_recv()
    lift_x = [
        second(0, 5 + i, s["liftf"].at[:, x, lift_rows, :], at_x(i)) for i in range(1, 4)
    ]
    for copy in out_x:
        copy.wait_recv()
    out_y = [
        second(1, 5 + i, s["outf"].at[:, :, out_rows, out_cols(y)], at_y(i)) for i in range(1, 4)
    ]
    lift_core, out_core = [lift_to_core(0)], [out_to_core(0)]

    got_gate()
    gating = dot(s["emb"][...].astype(BF16), s["gcols"][...], ((1,), (0,)))[0:1]
    got_q()
    got_k()
    got_v()
    send_mix, got_mix = head_to_tok(3, s["gated"], s["mix_tok"])

    def forward(i, _):
        block = lax.rem(lax.div(me, 2) + i, LEN // QB)
        at = pl.ds(pl.multiple_of(block * QB, QB), QB)
        scores = dot(s["qh"][at, :], s["kh"][...], ((1,), (1,)))
        most = jnp.max(scores, axis=1, keepdims=True)
        shifted = jnp.exp2((scores - most) * LOG2)
        weight = jnp.sum(shifted, axis=1, keepdims=True)
        mixed = dot(shifted.astype(BF16), s["vh"][...], ((1,), (0,))) / weight
        s["o32"][at, :] = mixed
        s["gated"][at, :] = (gating * mixed.astype(BF16).astype(F32)).astype(BF16)
        level = jnp.broadcast_to(most * LOG2 + jnp.log2(weight), (QB, 128))
        s["lse"][:, at] = jnp.transpose(level)[0:8]
        send_mix(2 * block)
        send_mix(2 * block + 1)
        return 0

    lax.fori_loop(0, LEN // QB, forward, 0)
    for i, copy in enumerate(lift_x):
        copy.wait_recv()
        lift_core.append(lift_to_core(i + 1))
    for i, copy in enumerate(out_y):
        copy.wait_recv()
        out_core.append(out_to_core(i + 1))

    got_mix()
    hidden = (res[...].astype(F32) + s["mix_tok"][...].astype(F32)).astype(BF16)
    s["hid2"][0:TOK, :] = hidden
    pair = [
        go(s["hid2"].at[0:TOK, :], s["hid2"].at[TOK:, :],
           s["s_pair"].at[0], s["r_pair"].at[0], partner)
    ]
    for copy in lift_core:
        copy.wait_recv()
    lifted = jnp.zeros((TOK, PH), F32)
    for i in range(4):
        lifted += dot(
            s["hid2"][0:TOK, i * 512 : (i + 1) * 512],
            s["liftf"][i].reshape(512, PH), ((1,), (0,)),
        )
    sigmoid = jax.nn.sigmoid(lifted)
    s["act2"][0:TOK, :] = (lifted * sigmoid).astype(BF16)
    slope = sigmoid * (1.0 + lifted * (1.0 - sigmoid))
    pair.append(
        go(s["act2"].at[0:TOK, :], s["act2"].at[TOK:, :],
           s["s_pair"].at[1], s["r_pair"].at[1], partner)
    )
    for copy in out_core:
        copy.wait_recv()
    predicted = jnp.zeros((TOK, ZD), F32)
    for i in range(4):
        predicted += dot(
            s["act2"][0:TOK, i * 256 : (i + 1) * 256],
            s["outf"][i].reshape(256, ZD), ((1,), (0,)),
        )
    def relay_wait(i, _):
        j = lax.rem(me + i, 16)
        relay(j, j).wait_recv()
        return 0

    relay_own.wait()
    lax.fori_loop(1, 16, relay_wait, 0)
    tokens = lax.broadcasted_iota(jnp.int32, (256, TOK), 1).astype(F32) + 1.0
    placed = jnp.where(s["rows_got"][:, ZD : ZD + 1].astype(F32) == tokens, 1.0, 0.0).astype(BF16)
    target = dot(placed, s["rows_got"][:, :ZD], ((0,), (0,)))
    target_norm = jnp.sqrt(jnp.sum(target * target, axis=1, keepdims=True) + EPSILON)

    pred_norm = jnp.sqrt(jnp.sum(predicted * predicted, axis=1, keepdims=True) + EPSILON)
    both = pred_norm * target_norm
    cosine = jnp.sum(predicted * target, axis=1, keepdims=True) / both
    grad_pred = (
        (-1.0 * ZD) * (target / both - cosine * predicted / (pred_norm * pred_norm))
    ).astype(BF16)
    s["gpf"][0] = grad_pred[:, : ZD // 2]
    s["gpf"][1] = grad_pred[:, ZD // 2 :]
    pair.append(
        go(s["gpf"].at[1 - c], s["gp2"].at[TOK:, :], s["s_pair"].at[2], s["r_pair"].at[2], partner)
    )
    for i in range(4):
        at = slice(i * 256, (i + 1) * 256)
        grad_act = dot(grad_pred, s["outf"][i].reshape(256, ZD), ((1,), (1,)))
        s["glf"][i // 2, :, (i % 2) * 256 : (i % 2 + 1) * 256] = (
            grad_act * slope[:, at]
        ).astype(BF16)
    pair.append(
        go(s["glf"].at[1 - c], s["gl2"].at[TOK:, :], s["s_pair"].at[3], s["r_pair"].at[3], partner)
    )
    grad_lifted = jnp.concatenate([s["glf"][0], s["glf"][1]], axis=1)
    s["glw"][...] = grad_lifted
    _, _, send_grad, got_grad = tok_to_head(4, s["ghs"], s["gh"])

    def hidden_part(i, _):
        group = lax.rem(lax.div(me, 4) + i, 4)
        s["ghs"][:, pl.ds(pl.multiple_of(group * 512, 512), 512)] = dot(
            s["glw"][...], s["liftf"][group].reshape(512, PH), ((1,), (1,))
        ).astype(BF16)
        for r in range(4):
            send_grad(group * 4 + lax.rem(me + r, 4))
        return 0

    lax.fori_loop(0, 4, hidden_part, 0)

    s["gp2"][0:TOK, :] = s["gpf"][c]
    s["gl2"][0:TOK, :] = s["glf"][c]
    for copy in pair:
        copy.wait_recv()

    def lift_part(i, _):
        s["gl_x"][lax.div(i, 4), lax.rem(i, 4)] = dot(
            s["hid2"][:, cols(i)], s["gl2"][...], ((0,), (0,))
        ).astype(BF16)
        return 0

    lax.fori_loop(0, 16, lift_part, 0)

    def out_part(i, _):
        done = dot(s["act2"][:, cols(i)], s["gp2"][...], ((0,), (0,))).astype(BF16)
        first = 2 * i
        s["go_x"][lax.div(first, 4), lax.rem(first, 4)] = done[:64]
        s["go_x"][lax.div(first, 4), lax.rem(first, 4) + 1] = done[64:]
        return 0

    lax.fori_loop(0, 8, out_part, 0)
    sums = []
    for i in range(1, 4):
        rows = pl.ds(pl.multiple_of(lax.rem(y + i, 4) * 16, 16), 16)
        sums.append(
            go(s["gl_x"].at[:, lax.rem(x + i, 4)], s["rl_x"].at[i - 1],
               s["s_red"].at[0, i - 1], s["r_red"].at[0, i - 1], at_x(i))
        )
        sums.append(
            go(s["go_x"].at[:, :, rows, :], s["ro_y"].at[i - 1],
               s["s_red"].at[1, i - 1], s["r_red"].at[1, i - 1], at_y(i))
        )

    def total(own, room):
        added = own.astype(F32)
        for i in range(room.shape[0]):
            added += room[i].astype(F32)
        return added

    got_grad()
    ones = jnp.ones((8, HD), BF16)

    def prepare(i, partial):
        at = pl.ds(pl.multiple_of(i * QB, QB), QB)
        grad = s["gh"][at, :].astype(F32)
        mixed = s["o32"][at, :]
        scaled = (gating * grad).astype(BF16)
        s["do"][at, :] = scaled
        inner = scaled.astype(F32) * mixed
        upper = inner.astype(BF16)
        lower = (inner - upper.astype(F32)).astype(BF16)
        s["drow"][:, at] = dot(ones, upper, ((1,), (1,))) + dot(ones, lower, ((1,), (1,)))
        product = grad * mixed.astype(BF16).astype(F32)
        return partial + jnp.sum(product.reshape(QB // 8, 8, HD), axis=0)

    s["ggs"][...] = lax.fori_loop(0, LEN // QB, prepare, jnp.zeros((8, HD), F32))
    got_gg = spread(2, lambda j: s["ggs"], lambda j: s["ggall"].at[j], dp, lambda j: (j, me))
    s["dq32"][...] = jnp.zeros((LEN, HD), F32)
    send_dk, got_dk = head_to_tok(5, s["dkb"], dk)
    send_dv, got_dv = head_to_tok(6, s["dvb"], dv)
    send_dq, got_dq = head_to_tok(7, s["dqb"], dq)

    def backward(i, _):
        block = lax.rem(lax.div(me, 2) + i, LEN // KB)
        at = pl.ds(pl.multiple_of(block * KB, KB), KB)
        keys = s["kh"][at, :]
        scores = dot(keys, s["qh"][...], ((1,), (1,)))
        chances = jnp.exp2(scores * LOG2 - s["lse"][0:1, :])
        s["dvb"][at, :] = dot(chances.astype(BF16), s["do"][...], ((1,), (0,))).astype(BF16)
        grad_chances = dot(s["vh"][at, :], s["do"][...], ((1,), (1,)))
        grad_scores = (chances * (grad_chances - s["drow"][0:1, :])).astype(BF16)
        s["dkb"][at, :] = (dot(grad_scores, s["qh"][...], ((1,), (0,))) * SCALE).astype(BF16)
        for send in (send_dv, send_dk):
            send(2 * block)
            send(2 * block + 1)
        s["dq32"][...] += dot(grad_scores, keys, ((0,), (0,)))
        return 0

    lax.fori_loop(0, EARLY, backward, 0)

    got_emb()
    got_gg()
    s["gfull"][...] = dot(
        s["embs"][...].reshape(128, TEMB), s["ggall"][...].reshape(128, HD), ((0,), (0,)),
        lax.Precision.HIGHEST,
    )
    s["gsl"][...] = s["gfull"][pl.ds(pl.multiple_of(dp * 16, 16), 16), :]
    got_ggate = spread(
        3, lambda j: s["gsl"], lambda j: ggate.at[:, cols(j)], me, lambda j: (dp, j)
    )

    for copy in sums:
        copy.wait_recv()
    s["gl_y"][...] = total(s["gl_x"][:, x], s["rl_x"]).astype(BF16)
    y_rows = pl.ds(pl.multiple_of(y * 16, 16), 16)
    s["go_y"][...] = total(s["go_x"][:, :, y_rows, :], s["ro_y"]).astype(BF16)
    sums = []
    for i in range(1, 4):
        rows = pl.ds(pl.multiple_of(lax.rem(y + i, 4) * 32, 32), 32)
        sums.append(
            go(s["gl_y"].at[:, rows, :], s["rl_y"].at[i - 1],
               s["s_red"].at[0, 2 + i], s["r_red"].at[0, 2 + i], at_y(i))
        )
        sums.append(
            go(s["go_y"].at[:, lax.rem(x + i, 4)], s["ro_x"].at[i - 1],
               s["s_red"].at[1, 2 + i], s["r_red"].at[1, 2 + i], at_x(i))
        )
    lax.fori_loop(EARLY, LEN // KB, backward, 0)
    for copy in sums:
        copy.wait_recv()
    y_rows = pl.ds(pl.multiple_of(y * 32, 32), 32)
    s["gl_z"][...] = total(s["gl_y"][:, y_rows, :], s["rl_y"]).astype(BF16)
    s["go_z"][...] = total(s["go_y"][:, x], s["ro_x"]).astype(BF16)
    sums = []
    for n, (part, room) in enumerate([("gl_z", "rl_z"), ("go_z", "ro_z")]):
        for i, hop in enumerate((1, 7, 2 + 4 * c)):
            sums.append(
                go(s[part].at[lax.rem(z + hop, 4)], s[room].at[i],
                   s["s_red"].at[n, 6 + i], s["r_red"].at[n, 6 + i], at_z(hop))
            )

    s["dqb"][...] = (s["dq32"][...] * SCALE).astype(BF16)

    def send_queries(i, _):
        half = lax.rem(1 - zh + lax.div(i, 8), 2)
        send_dq(half * 8 + lax.rem(yc + i, 8))
        return 0

    lax.fori_loop(0, 16, send_queries, 0)

    for copy in sums:
        copy.wait_recv()
    sums = []
    halves = [("gl_z", "rl_z", "hl_z"), ("go_z", "ro_z", "ho_z")]
    for n, (part, room, side) in enumerate(halves):
        s[side][0] = total(s[part][zl], s[room]).astype(BF16)
        sums.append(
            go(s[side].at[0], s[side].at[1], s["s_red"].at[n, 9], s["r_red"].at[n, 9], at_z(4))
        )
    for copy in sums:
        copy.wait_recv()
    sums = []
    final = [
        ("hl_z", "pl_f", "lift_sum", 32, PH // 2),
        ("ho_z", "po_f", "out_sum", 16, ZD // 2),
    ]
    for n, (side, piece, whole, height, width) in enumerate(final):
        added = (s[side][0].astype(F32) + s[side][1].astype(F32)).astype(BF16)
        s[piece][...] = added
        rows = pl.ds(pl.multiple_of(y * height, height), height)
        part = pl.ds(pl.multiple_of(c * width, 128), width)
        s[whole][rows, part] = added
        for i in range(1, 8):
            sums.append(
                go(s[piece], s[whole].at[rows, part],
                   s["s_red"].at[n, 12 + i], s["r_red"].at[n, 12 + i], at_yc(i))
            )
    got_ggate()
    for copy in sums:
        copy.wait_recv()
    for whole, out, n in (("lift_sum", glift, 15), ("out_sum", gout, 16)):
        own = pltpu.make_async_copy(s[whole], out, s["local"].at[n])
        own.start()
        finish.append(own.wait)
    got_dk()
    got_dv()
    got_dq()
    for wait in finish:
        wait()


def copy_kernel(*refs):
    for i in range(6):
        refs[6 + i][...] = refs[i][...].astype(refs[6 + i].dtype)


def shards(
    queries,
    key_states,
    value_states,
    residual,
    enc_hidden,
    enc_gain,
    enc_bias,
    feature_target,
    timestep,
    gate_weight,
    lift_weight,
    out_weight,
):
    anywhere = pl.BlockSpec(memory_space=pl.ANY)
    near = pl.BlockSpec(memory_space=pltpu.VMEM)
    tok = jax.ShapeDtypeStruct((TOK, FEAT), BF16)
    out_shape = (
        tok, tok, tok,
        jax.ShapeDtypeStruct((16, FEAT), F32),
        jax.ShapeDtypeStruct((128, PH), F32),
        jax.ShapeDtypeStruct((64, ZD), F32),
    )
    outs = pl.pallas_call(
        step_kernel,
        out_shape=out_shape[:4]
        + (jax.ShapeDtypeStruct((128, PH), BF16), jax.ShapeDtypeStruct((64, ZD), BF16)),
        in_specs=[anywhere] * 3 + [near] * 5 + [pl.BlockSpec(memory_space=pltpu.SMEM)]
        + [anywhere] * 3,
        out_specs=(anywhere,) * 6,
        scratch_shapes=list(SCRATCH.values()),
        compiler_params=pltpu.CompilerParams(
            collective_id=0, has_side_effects=True, vmem_limit_bytes=60 << 20
        ),
        name="repa_step",
    )(
        queries[0], key_states[0], value_states[0], residual[0], enc_hidden[0],
        enc_gain, enc_bias, feature_target, timestep, gate_weight, lift_weight, out_weight,
    )
    d_queries, d_keys, d_values, grad_gate, grad_lift, grad_out = pl.pallas_call(
        copy_kernel,
        out_shape=out_shape,
        grid=(2,),
        in_specs=[pl.BlockSpec((a.shape[0] // 2, a.shape[1]), lambda i: (i, 0)) for a in out_shape],
        out_specs=[pl.BlockSpec((a.shape[0] // 2, a.shape[1]), lambda i: (i, 0)) for a in out_shape],
        compiler_params=pltpu.CompilerParams(vmem_limit_bytes=60 << 20),
        name="hand_out",
    )(*outs)
    return (d_queries[None], d_keys[None], d_values[None], grad_gate, grad_lift, grad_out)


def solution(mesh):
    tokens = P("dp", "seq", None)
    rows = P("dp", None)
    in_specs = (tokens,) * 5 + (P(), P(), P("dp", "seq"), P("dp"), rows, rows, rows)
    out_specs = (tokens,) * 3 + (rows,) * 3
    return jax.shard_map(
        shards, mesh=mesh, in_specs=in_specs, out_specs=out_specs, check_vma=False
    )
```

```python
import functools
import math

import jax
import jax.numpy as jnp
from jax import lax
from jax.experimental import pallas as pl
from jax.experimental.pallas import tpu as pltpu
from jax.sharding import PartitionSpec as P

HD = 128
ZD = 1536
PH = 1024
FEAT = 2048
TEMB = 256
LEN = 2048
TOK = 128
EPSILON = 1e-06
SCALE = HD ** (-0.5)
LOG2 = SCALE * math.log2(math.e)
QB = 256
KB = 256
EARLY = 7
MESH = pl.DeviceIdType.MESH
F32 = jnp.float32
BF16 = jnp.bfloat16

SCRATCH = dict(
    qh=pltpu.VMEM((LEN, HD), BF16),
    kh=pltpu.VMEM((LEN, HD), BF16),
    vh=pltpu.VMEM((LEN, HD), BF16),
    gcols=pltpu.VMEM((TEMB, HD), BF16),
    emb=pltpu.VMEM((8, TEMB), F32),
    embs=pltpu.VMEM((16, 8, TEMB), F32),
    rows_send=pltpu.VMEM((256, ZD + 128), BF16),
    rows_got=pltpu.VMEM((256, ZD + 128), BF16),
    liftf=pltpu.VMEM((4, 4, 128, PH), BF16),
    outf=pltpu.VMEM((4, 4, 64, ZD), BF16),
    o32=pltpu.VMEM((LEN, HD), F32),
    lse=pltpu.VMEM((8, LEN), F32),
    gated=pltpu.VMEM((LEN, HD), BF16),
    mix_tok=pltpu.VMEM((TOK, FEAT), BF16),
    hid2=pltpu.VMEM((2 * TOK, FEAT), BF16),
    act2=pltpu.VMEM((2 * TOK, PH), BF16),
    gpf=pltpu.VMEM((2, TOK, ZD // 2), BF16),
    gp2=pltpu.VMEM((2 * TOK, ZD // 2), BF16),
    glf=pltpu.VMEM((2, TOK, PH // 2), BF16),
    gl2=pltpu.VMEM((2 * TOK, PH // 2), BF16),
    glw=pltpu.VMEM((TOK, PH), BF16),
    ghs=pltpu.VMEM((TOK, FEAT), BF16),
    gh=pltpu.VMEM((LEN, HD), BF16),
    do=pltpu.VMEM((LEN, HD), BF16),
    drow=pltpu.VMEM((8, LEN), F32),
    dq32=pltpu.VMEM((LEN, HD), F32),
    dqb=pltpu.VMEM((LEN, HD), BF16),
    dkb=pltpu.VMEM((LEN, HD), BF16),
    dvb=pltpu.VMEM((LEN, HD), BF16),
    ggs=pltpu.VMEM((8, HD), F32),
    ggall=pltpu.VMEM((16, 8, HD), F32),
    gfull=pltpu.VMEM((TEMB, HD), F32),
    gsl=pltpu.VMEM((16, HD), F32),
    gl_x=pltpu.VMEM((4, 4, 128, PH // 2), BF16),
    go_x=pltpu.VMEM((4, 4, 64, ZD // 2), BF16),
    rl_x=pltpu.VMEM((3, 4, 128, PH // 2), BF16),
    ro_y=pltpu.VMEM((3, 4, 4, 16, ZD // 2), BF16),
    gl_y=pltpu.VMEM((4, 128, PH // 2), BF16),
    go_y=pltpu.VMEM((4, 4, 16, ZD // 2), BF16),
    rl_y=pltpu.VMEM((3, 4, 32, PH // 2), BF16),
    ro_x=pltpu.VMEM((3, 4, 16, ZD // 2), BF16),
    gl_z=pltpu.VMEM((4, 32, PH // 2), BF16),
    go_z=pltpu.VMEM((4, 16, ZD // 2), BF16),
    rl_z=pltpu.VMEM((3, 32, PH // 2), BF16),
    ro_z=pltpu.VMEM((3, 16, ZD // 2), BF16),
    hl_z=pltpu.VMEM((2, 32, PH // 2), BF16),
    ho_z=pltpu.VMEM((2, 16, ZD // 2), BF16),
    pl_f=pltpu.VMEM((32, PH // 2), BF16),
    po_f=pltpu.VMEM((16, ZD // 2), BF16),
    lift_sum=pltpu.VMEM((128, PH), BF16),
    out_sum=pltpu.VMEM((64, ZD), BF16),
    s_a2a=pltpu.SemaphoreType.DMA((8, 16)),
    r_a2a=pltpu.SemaphoreType.DMA((8, 16)),
    s_rel=pltpu.SemaphoreType.DMA((16,)),
    r_rel=pltpu.SemaphoreType.DMA((16,)),
    s_gate=pltpu.SemaphoreType.DMA((4, 16)),
    r_gate=pltpu.SemaphoreType.DMA((4, 16)),
    s_w=pltpu.SemaphoreType.DMA((2, 13)),
    r_w=pltpu.SemaphoreType.DMA((2, 13)),
    s_pair=pltpu.SemaphoreType.DMA((4,)),
    r_pair=pltpu.SemaphoreType.DMA((4,)),
    s_red=pltpu.SemaphoreType.DMA((2, 20)),
    r_red=pltpu.SemaphoreType.DMA((2, 20)),
    local=pltpu.SemaphoreType.DMA((20,)),
)
NAMES = list(SCRATCH)


def dot(a, b, dims, precision=None):
    return lax.dot_general(
        a, b, (dims, ((), ())), precision=precision, preferred_element_type=F32
    )


def step_kernel(*refs):
    q, k, v, res, enc, gain, bias, trow, when, gate, lift, outw = refs[:12]
    dq, dk, dv, ggate, glift, gout = refs[12:18]
    s = dict(zip(NAMES, refs[18:]))
    dp, me = lax.axis_index("dp"), lax.axis_index("seq")
    zl, x = lax.div(dp, 4), lax.rem(dp, 4)
    zh, yc = lax.div(me, 8), lax.rem(me, 8)
    y, c = lax.div(yc, 2), lax.rem(yc, 2)
    z = zh * 4 + zl
    partner = (dp, me + 1 - 2 * c)

    def at_x(i):
        return (zl * 4 + lax.rem(x + i, 4), me)

    def at_y(i):
        return (dp, zh * 8 + lax.rem(y + i, 4) * 2 + c)

    def at_z(i):
        to = lax.rem(z + i, 8)
        return (lax.rem(to, 4) * 4 + x, lax.div(to, 4) * 8 + yc)

    def at_yc(i):
        return (dp, zh * 8 + lax.rem(yc + i, 8))

    def cols(j):
        return pl.ds(pl.multiple_of(j * 128, 128), 128)

    def remote(src, dst, send, recv, device):
        return pltpu.make_async_remote_copy(
            src_ref=src, dst_ref=dst, send_sem=send, recv_sem=recv,
            device_id=device, device_id_type=MESH,
        )

    finish = []

    def go(*copy):
        made = remote(*copy)
        made.start()
        finish.append(made.wait_send)
        return made

    half = TEMB // 2
    index = lax.broadcasted_iota(jnp.int32, (8, half), 1).astype(F32)
    angles = when[0].astype(F32) * jnp.exp(-math.log(10000.0) * index / half)
    s["emb"][:, :half] = jnp.cos(angles).astype(BF16).astype(F32)
    s["emb"][:, half:] = jnp.sin(angles).astype(BF16).astype(F32)

    barrier = pltpu.get_barrier_semaphore()

    def greet(i, _):
        pl.semaphore_signal(barrier, 1, device_id=(dp, lax.rem(me + i, 16)), device_id_type=MESH)
        pl.semaphore_signal(barrier, 1, device_id=(lax.rem(dp + i, 16), me), device_id_type=MESH)
        return 0

    lax.fori_loop(1, 16, greet, 0)
    for i in range(1, 4):
        other = (lax.rem(zl + i, 4) * 4 + x, (1 - zh) * 8 + yc)
        pl.semaphore_signal(barrier, 1, device_id=other, device_id_type=MESH)
    pl.semaphore_wait(barrier, 33)

    def tok_to_head(t, src, dst):
        def copy(j, owner):
            return remote(
                src.at[:, cols(j)], dst.at[cols(owner), :],
                s["s_a2a"].at[t, j], s["r_a2a"].at[t, owner], (dp, j),
            )

        def far(i, _):
            copy(lax.rem(me + i + 8, 16), me).start()
            return 0

        def near(i, _):
            copy(lax.rem(me + i, 16), me).start()
            return 0

        own = pltpu.make_async_copy(src.at[:, cols(me)], dst.at[cols(me), :], s["local"].at[t])

        def send(j):
            @pl.when(j != me)
            def _():
                copy(j, me).start()

            @pl.when(j == me)
            def _():
                own.start()

        def start_far():
            lax.fori_loop(0, 8, far, 0)

        def start_near():
            own.start()
            lax.fori_loop(1, 8, near, 0)

        def wait():
            def one(i, _):
                j = lax.rem(me + i, 16)
                copy(j, j).wait_recv()
                return 0

            own.wait()
            lax.fori_loop(1, 16, one, 0)

        def sent():
            def one(i, _):
                copy(lax.rem(me + i, 16), me).wait_send()
                return 0

            lax.fori_loop(1, 16, one, 0)

        finish.append(sent)
        return start_far, start_near, send, wait

    def head_to_tok(t, src, dst):
        def copy(j, owner):
            return remote(
                src.at[cols(j), :], dst.at[:, cols(owner)],
                s["s_a2a"].at[t, j], s["r_a2a"].at[t, owner], (dp, j),
            )

        own = pltpu.make_async_copy(src.at[cols(me), :], dst.at[:, cols(me)], s["local"].at[t])

        def send(j):
            @pl.when(j != me)
            def _():
                copy(j, me).start()

            @pl.when(j == me)
            def _():
                own.start()

        def wait():
            def one(i, _):
                j = lax.rem(me + i, 16)
                copy(j, j).wait_recv()
                return 0

            own.wait()
            lax.fori_loop(1, 16, one, 0)

        def sent():
            def one(i, _):
                copy(lax.rem(me + i, 16), me).wait_send()
                return 0

            lax.fori_loop(1, 16, one, 0)

        finish.append(sent)
        return send, wait

    def spread(t, src_of, dst_of, index, device_of):
        def copy(j, owner):
            return remote(
                src_of(j), dst_of(owner), s["s_gate"].at[t, j], s["r_gate"].at[t, owner],
                device_of(j),
            )

        def start(i, _):
            copy(lax.rem(index + i, 16), index).start()
            return 0

        own = pltpu.make_async_copy(src_of(index), dst_of(index), s["local"].at[8 + t])
        own.start()
        lax.fori_loop(1, 16, start, 0)

        def wait():
            def one(i, _):
                j = lax.rem(index + i, 16)
                copy(j, j).wait_recv()
                return 0

            own.wait()
            lax.fori_loop(1, 16, one, 0)

        def sent():
            def one(i, _):
                copy(lax.rem(index + i, 16), index).wait_send()
                return 0

            lax.fori_loop(1, 16, one, 0)

        finish.append(sent)
        return wait

    weights = [(lift, s["liftf"], 64, 256), (outw, s["outf"], 32, 384)]
    z_hops = [at_z(1), at_z(7), at_z(2 + 4 * c)]
    along_z = []
    for n, (shard, full, height, width) in enumerate(weights):
        rows = pl.ds(pl.multiple_of(c * height, height), height)
        part = pl.ds(pl.multiple_of(y * width, 128), width)
        for i, device in enumerate(z_hops):
            along_z.append(
                go(shard.at[rows, part], full.at[zl, x, rows, part],
                   s["s_w"].at[n, i], s["r_w"].at[n, i], device).wait_recv
            )
        own = pltpu.make_async_copy(
            shard.at[rows, part], full.at[zl, x, rows, part], s["local"].at[12 + n]
        )
        own.start()
        along_z.append(own.wait)
    far_q, near_q, _, got_q = tok_to_head(0, q, s["qh"])
    far_k, near_k, _, got_k = tok_to_head(1, k, s["kh"])
    far_v, near_v, _, got_v = tok_to_head(2, v, s["vh"])
    for start in (near_q, far_q, near_k, far_k, near_v, far_v):
        start()
    got_gate = spread(
        0, lambda j: gate.at[:, cols(me)],
        lambda j: s["gcols"].at[pl.ds(pl.multiple_of(j * 16, 16), 16), :], dp,
        lambda j: (j, me),
    )
    got_emb = spread(1, lambda j: s["emb"], lambda j: s["embs"].at[j], dp, lambda j: (j, me))

    wide = enc[...].astype(F32)
    centred = wide - jnp.mean(wide, axis=-1, keepdims=True)
    variance = jnp.mean(centred * centred, axis=-1, keepdims=True)
    normed = (centred * lax.rsqrt(variance + EPSILON) * gain[...][None] + bias[...][None]).astype(BF16)
    tcol = jnp.transpose(jnp.broadcast_to(trow[...], (TOK, TOK)))
    own_row, own_col = lax.shift_right_logical(trow[...], 7), lax.shift_right_logical(tcol, 7)
    before = lax.broadcasted_iota(jnp.int32, (TOK, TOK), 0) < lax.broadcasted_iota(
        jnp.int32, (TOK, TOK), 1
    )
    same = jnp.where((own_col == own_row) & before, 1.0, 0.0)
    slot = own_row.astype(F32) * 16.0 + jnp.sum(same, axis=0, keepdims=True)
    place = ((tcol & 127) + 1).astype(F32).astype(BF16)
    slots = lax.broadcasted_iota(jnp.int32, (256, TOK), 0).astype(F32)
    pick = jnp.where(slots == slot, 1.0, 0.0).astype(BF16)
    s["rows_send"][:, :ZD] = dot(pick, normed, ((1,), (0,))).astype(BF16)
    s["rows_send"][:, ZD:] = dot(pick, place, ((1,), (0,))).astype(BF16)

    def relay(j, owner):
        return remote(
            s["rows_send"].at[pl.ds(pl.multiple_of(j * 16, 16), 16), :],
            s["rows_got"].at[pl.ds(pl.multiple_of(owner * 16, 16), 16), :],
            s["s_rel"].at[j], s["r_rel"].at[owner], (dp, j),
        )

    def relay_near(i, _):
        relay(zh * 8 + lax.rem(yc + i, 8), me).start()
        return 0

    def relay_far(i, _):
        relay((1 - zh) * 8 + lax.rem(yc + i, 8), me).start()
        return 0

    def relay_sent():
        def one(i, _):
            relay(lax.rem(me + i, 16), me).wait_send()
            return 0

        lax.fori_loop(1, 16, one, 0)

    finish.append(relay_sent)

    lax.fori_loop(1, 8, relay_near, 0)
    lax.fori_loop(0, 8, relay_far, 0)
    mine = pl.ds(pl.multiple_of(me * 16, 16), 16)
    relay_own = pltpu.make_async_copy(
        s["rows_send"].at[mine, :], s["rows_got"].at[mine, :], s["local"].at[14]
    )
    relay_own.start()

    for wait in along_z:
        wait()
    def second(n, i, piece, device):
        return go(piece, piece, s["s_w"].at[n, i], s["r_w"].at[n, i], device)

    lift_rows = pl.ds(pl.multiple_of(c * 64, 64), 64)
    out_rows = pl.ds(pl.multiple_of(c * 32, 32), 32)

    def lift_cols(at):
        return pl.ds(pl.multiple_of(lax.rem(at, 4) * 256, 128), 256)

    def out_cols(at):
        return pl.ds(pl.multiple_of(lax.rem(at, 4) * 384, 128), 384)

    lift_y = [
        second(0, 2 + i, s["liftf"].at[:, x, lift_rows, lift_cols(y)], at_y(i))
        for i in range(1, 4)
    ]
    out_x = [
        second(1, 2 + i, s["outf"].at[:, x, out_rows, out_cols(y)], at_x(i))
        for i in range(1, 4)
    ]

    def lift_to_core(i):
        return second(0, 9 + i, s["liftf"].at[:, lax.rem(x + 4 - i, 4), lift_rows, :], partner)

    def out_to_core(i):
        return second(1, 9 + i, s["outf"].at[:, :, out_rows, out_cols(y + 4 - i)], partner)

    for copy in lift_y:
        copy.wait_recv()
    lift_x = [
        second(0, 5 + i, s["liftf"].at[:, x, lift_rows, :], at_x(i)) for i in range(1, 4)
    ]
    for copy in out_x:
        copy.wait_recv()
    out_y = [
        second(1, 5 + i, s["outf"].at[:, :, out_rows, out_cols(y)], at_y(i)) for i in range(1, 4)
    ]
    lift_core, out_core = [lift_to_core(0)], [out_to_core(0)]

    got_gate()
    gating = dot(s["emb"][...].astype(BF16), s["gcols"][...], ((1,), (0,)))[0:1]
    got_q()
    got_k()
    got_v()
    send_mix, got_mix = head_to_tok(3, s["gated"], s["mix_tok"])

    def forward(i, _):
        block = lax.rem(lax.div(me, 2) + i, LEN // QB)
        at = pl.ds(pl.multiple_of(block * QB, QB), QB)
        scores = dot(s["qh"][at, :], s["kh"][...], ((1,), (1,)))
        most = jnp.max(scores, axis=1, keepdims=True)
        shifted = jnp.exp2((scores - most) * LOG2)
        weight = jnp.sum(shifted, axis=1, keepdims=True)
        mixed = dot(shifted.astype(BF16), s["vh"][...], ((1,), (0,))) / weight
        s["o32"][at, :] = mixed
        s["gated"][at, :] = (gating * mixed.astype(BF16).astype(F32)).astype(BF16)
        level = jnp.broadcast_to(most * LOG2 + jnp.log2(weight), (QB, 128))
        s["lse"][:, at] = jnp.transpose(level)[0:8]
        send_mix(2 * block)
        send_mix(2 * block + 1)
        return 0

    lax.fori_loop(0, LEN // QB, forward, 0)
    for i, copy in enumerate(lift_x):
        copy.wait_recv()
        lift_core.append(lift_to_core(i + 1))
    for i, copy in enumerate(out_y):
        copy.wait_recv()
        out_core.append(out_to_core(i + 1))

    got_mix()
    hidden = (res[...].astype(F32) + s["mix_tok"][...].astype(F32)).astype(BF16)
    s["hid2"][0:TOK, :] = hidden
    pair = [
        go(s["hid2"].at[0:TOK, :], s["hid2"].at[TOK:, :],
           s["s_pair"].at[0], s["r_pair"].at[0], partner)
    ]
    for copy in lift_core:
        copy.wait_recv()
    lifted = jnp.zeros((TOK, PH), F32)
    for i in range(4):
        lifted += dot(
            s["hid2"][0:TOK, i * 512 : (i + 1) * 512],
            s["liftf"][i].reshape(512, PH), ((1,), (0,)),
        )
    sigmoid = jax.nn.sigmoid(lifted)
    s["act2"][0:TOK, :] = (lifted * sigmoid).astype(BF16)
    slope = sigmoid * (1.0 + lifted * (1.0 - sigmoid))
    pair.append(
        go(s["act2"].at[0:TOK, :], s["act2"].at[TOK:, :],
           s["s_pair"].at[1], s["r_pair"].at[1], partner)
    )
    for copy in out_core:
        copy.wait_recv()
    predicted = jnp.zeros((TOK, ZD), F32)
    for i in range(4):
        predicted += dot(
            s["act2"][0:TOK, i * 256 : (i + 1) * 256],
            s["outf"][i].reshape(256, ZD), ((1,), (0,)),
        )
    def relay_wait(i, _):
        j = lax.rem(me + i, 16)
        relay(j, j).wait_recv()
        return 0

    relay_own.wait()
    lax.fori_loop(1, 16, relay_wait, 0)
    tokens = lax.broadcasted_iota(jnp.int32, (256, TOK), 1).astype(F32) + 1.0
    placed = jnp.where(s["rows_got"][:, ZD : ZD + 1].astype(F32) == tokens, 1.0, 0.0).astype(BF16)
    target = dot(placed, s["rows_got"][:, :ZD], ((0,), (0,)))
    target_norm = jnp.sqrt(jnp.sum(target * target, axis=1, keepdims=True) + EPSILON)

    pred_norm = jnp.sqrt(jnp.sum(predicted * predicted, axis=1, keepdims=True) + EPSILON)
    both = pred_norm * target_norm
    cosine = jnp.sum(predicted * target, axis=1, keepdims=True) / both
    grad_pred = (
        (-1.0 * ZD) * (target / both - cosine * predicted / (pred_norm * pred_norm))
    ).astype(BF16)
    s["gpf"][0] = grad_pred[:, : ZD // 2]
    s["gpf"][1] = grad_pred[:, ZD // 2 :]
    pair.append(
        go(s["gpf"].at[1 - c], s["gp2"].at[TOK:, :], s["s_pair"].at[2], s["r_pair"].at[2], partner)
    )
    for i in range(4):
        at = slice(i * 256, (i + 1) * 256)
        grad_act = dot(grad_pred, s["outf"][i].reshape(256, ZD), ((1,), (1,)))
        s["glf"][i // 2, :, (i % 2) * 256 : (i % 2 + 1) * 256] = (
            grad_act * slope[:, at]
        ).astype(BF16)
    pair.append(
        go(s["glf"].at[1 - c], s["gl2"].at[TOK:, :], s["s_pair"].at[3], s["r_pair"].at[3], partner)
    )
    grad_lifted = jnp.concatenate([s["glf"][0], s["glf"][1]], axis=1)
    s["glw"][...] = grad_lifted
    _, _, send_grad, got_grad = tok_to_head(4, s["ghs"], s["gh"])

    def hidden_part(i, _):
        group = lax.rem(lax.div(me, 4) + i, 4)
        s["ghs"][:, pl.ds(pl.multiple_of(group * 512, 512), 512)] = dot(
            s["glw"][...], s["liftf"][group].reshape(512, PH), ((1,), (1,))
        ).astype(BF16)
        for r in range(4):
            send_grad(group * 4 + lax.rem(me + r, 4))
        return 0

    lax.fori_loop(0, 4, hidden_part, 0)

    s["gp2"][0:TOK, :] = s["gpf"][c]
    s["gl2"][0:TOK, :] = s["glf"][c]
    for copy in pair:
        copy.wait_recv()

    def lift_part(i, _):
        s["gl_x"][lax.div(i, 4), lax.rem(i, 4)] = dot(
            s["hid2"][:, cols(i)], s["gl2"][...], ((0,), (0,))
        ).astype(BF16)
        return 0

    lax.fori_loop(0, 16, lift_part, 0)

    def out_part(i, _):
        done = dot(s["act2"][:, cols(i)], s["gp2"][...], ((0,), (0,))).astype(BF16)
        first = 2 * i
        s["go_x"][lax.div(first, 4), lax.rem(first, 4)] = done[:64]
        s["go_x"][lax.div(first, 4), lax.rem(first, 4) + 1] = done[64:]
        return 0

    lax.fori_loop(0, 8, out_part, 0)
    sums = []
    for i in range(1, 4):
        rows = pl.ds(pl.multiple_of(lax.rem(y + i, 4) * 16, 16), 16)
        sums.append(
            go(s["gl_x"].at[:, lax.rem(x + i, 4)], s["rl_x"].at[i - 1],
               s["s_red"].at[0, i - 1], s["r_red"].at[0, i - 1], at_x(i))
        )
        sums.append(
            go(s["go_x"].at[:, :, rows, :], s["ro_y"].at[i - 1],
               s["s_red"].at[1, i - 1], s["r_red"].at[1, i - 1], at_y(i))
        )

    def total(own, room):
        added = own.astype(F32)
        for i in range(room.shape[0]):
            added += room[i].astype(F32)
        return added

    got_grad()
    ones = jnp.ones((8, HD), BF16)

    def prepare(i, partial):
        at = pl.ds(pl.multiple_of(i * QB, QB), QB)
        grad = s["gh"][at, :].astype(F32)
        mixed = s["o32"][at, :]
        scaled = (gating * grad).astype(BF16)
        s["do"][at, :] = scaled
        inner = scaled.astype(F32) * mixed
        upper = inner.astype(BF16)
        lower = (inner - upper.astype(F32)).astype(BF16)
        s["drow"][:, at] = dot(ones, upper, ((1,), (1,))) + dot(ones, lower, ((1,), (1,)))
        product = grad * mixed.astype(BF16).astype(F32)
        return partial + jnp.sum(product.reshape(QB // 8, 8, HD), axis=0)

    s["ggs"][...] = lax.fori_loop(0, LEN // QB, prepare, jnp.zeros((8, HD), F32))
    got_gg = spread(2, lambda j: s["ggs"], lambda j: s["ggall"].at[j], dp, lambda j: (j, me))
    s["dq32"][...] = jnp.zeros((LEN, HD), F32)
    send_dk, got_dk = head_to_tok(5, s["dkb"], dk)
    send_dv, got_dv = head_to_tok(6, s["dvb"], dv)
    send_dq, got_dq = head_to_tok(7, s["dqb"], dq)

    def backward(i, _):
        block = lax.rem(lax.div(me, 2) + i, LEN // KB)
        at = pl.ds(pl.multiple_of(block * KB, KB), KB)
        keys = s["kh"][at, :]
        scores = dot(keys, s["qh"][...], ((1,), (1,)))
        chances = jnp.exp2(scores * LOG2 - s["lse"][0:1, :])
        s["dvb"][at, :] = dot(chances.astype(BF16), s["do"][...], ((1,), (0,))).astype(BF16)
        grad_chances = dot(s["vh"][at, :], s["do"][...], ((1,), (1,)))
        grad_scores = (chances * (grad_chances - s["drow"][0:1, :])).astype(BF16)
        s["dkb"][at, :] = (dot(grad_scores, s["qh"][...], ((1,), (0,))) * SCALE).astype(BF16)
        for send in (send_dv, send_dk):
            send(2 * block)
            send(2 * block + 1)
        s["dq32"][...] += dot(grad_scores, keys, ((0,), (0,)))
        return 0

    lax.fori_loop(0, EARLY, backward, 0)

    got_emb()
    got_gg()
    s["gfull"][...] = dot(
        s["embs"][...].reshape(128, TEMB), s["ggall"][...].reshape(128, HD), ((0,), (0,)),
        lax.Precision.HIGHEST,
    )
    s["gsl"][...] = s["gfull"][pl.ds(pl.multiple_of(dp * 16, 16), 16), :]
    got_ggate = spread(
        3, lambda j: s["gsl"], lambda j: ggate.at[:, cols(j)], me, lambda j: (dp, j)
    )

    for copy in sums:
        copy.wait_recv()
    s["gl_y"][...] = total(s["gl_x"][:, x], s["rl_x"]).astype(BF16)
    y_rows = pl.ds(pl.multiple_of(y * 16, 16), 16)
    s["go_y"][...] = total(s["go_x"][:, :, y_rows, :], s["ro_y"]).astype(BF16)
    sums = []
    for i in range(1, 4):
        rows = pl.ds(pl.multiple_of(lax.rem(y + i, 4) * 32, 32), 32)
        sums.append(
            go(s["gl_y"].at[:, rows, :], s["rl_y"].at[i - 1],
               s["s_red"].at[0, 2 + i], s["r_red"].at[0, 2 + i], at_y(i))
        )
        sums.append(
            go(s["go_y"].at[:, lax.rem(x + i, 4)], s["ro_x"].at[i - 1],
               s["s_red"].at[1, 2 + i], s["r_red"].at[1, 2 + i], at_x(i))
        )
    lax.fori_loop(EARLY, LEN // KB, backward, 0)
    s["dqb"][...] = (s["dq32"][...] * SCALE).astype(BF16)

    def send_queries(i, _):
        half = lax.rem(1 - zh + lax.div(i, 8), 2)
        send_dq(half * 8 + lax.rem(yc + i, 8))
        return 0

    lax.fori_loop(0, 16, send_queries, 0)

    for copy in sums:
        copy.wait_recv()
    y_rows = pl.ds(pl.multiple_of(y * 32, 32), 32)
    s["gl_z"][...] = total(s["gl_y"][:, y_rows, :], s["rl_y"]).astype(BF16)
    s["go_z"][...] = total(s["go_y"][:, x], s["ro_x"]).astype(BF16)
    sums = []
    for n, (part, room) in enumerate([("gl_z", "rl_z"), ("go_z", "ro_z")]):
        for i, hop in enumerate((1, 7, 2 + 4 * c)):
            sums.append(
                go(s[part].at[lax.rem(z + hop, 4)], s[room].at[i],
                   s["s_red"].at[n, 6 + i], s["r_red"].at[n, 6 + i], at_z(hop))
            )

    for copy in sums:
        copy.wait_recv()
    sums = []
    halves = [("gl_z", "rl_z", "hl_z"), ("go_z", "ro_z", "ho_z")]
    for n, (part, room, side) in enumerate(halves):
        s[side][0] = total(s[part][zl], s[room]).astype(BF16)
        sums.append(
            go(s[side].at[0], s[side].at[1], s["s_red"].at[n, 9], s["r_red"].at[n, 9], at_z(4))
        )
    for copy in sums:
        copy.wait_recv()
    sums = []
    final = [
        ("hl_z", "pl_f", "lift_sum", 32, PH // 2),
        ("ho_z", "po_f", "out_sum", 16, ZD // 2),
    ]
    for n, (side, piece, whole, height, width) in enumerate(final):
        added = (s[side][0].astype(F32) + s[side][1].astype(F32)).astype(BF16)
        s[piece][...] = added
        rows = pl.ds(pl.multiple_of(y * height, height), height)
        part = pl.ds(pl.multiple_of(c * width, 128), width)
        s[whole][rows, part] = added
        for i in range(1, 8):
            sums.append(
                go(s[piece], s[whole].at[rows, part],
                   s["s_red"].at[n, 12 + i], s["r_red"].at[n, 12 + i], at_yc(i))
            )
    got_ggate()
    for copy in sums:
        copy.wait_recv()
    for whole, out, n in (("lift_sum", glift, 15), ("out_sum", gout, 16)):
        own = pltpu.make_async_copy(s[whole], out, s["local"].at[n])
        own.start()
        finish.append(own.wait)
    got_dk()
    got_dv()
    got_dq()
    for wait in finish:
        wait()


def copy_kernel(*refs):
    for i in range(6):
        refs[6 + i][...] = refs[i][...].astype(refs[6 + i].dtype)


def shards(
    queries,
    key_states,
    value_states,
    residual,
    enc_hidden,
    enc_gain,
    enc_bias,
    feature_target,
    timestep,
    gate_weight,
    lift_weight,
    out_weight,
):
    anywhere = pl.BlockSpec(memory_space=pl.ANY)
    near = pl.BlockSpec(memory_space=pltpu.VMEM)
    tok = jax.ShapeDtypeStruct((TOK, FEAT), BF16)
    out_shape = (
        tok, tok, tok,
        jax.ShapeDtypeStruct((16, FEAT), F32),
        jax.ShapeDtypeStruct((128, PH), F32),
        jax.ShapeDtypeStruct((64, ZD), F32),
    )
    outs = pl.pallas_call(
        step_kernel,
        out_shape=out_shape[:4]
        + (jax.ShapeDtypeStruct((128, PH), BF16), jax.ShapeDtypeStruct((64, ZD), BF16)),
        in_specs=[anywhere] * 3 + [near] * 5 + [pl.BlockSpec(memory_space=pltpu.SMEM)]
        + [anywhere] * 3,
        out_specs=(anywhere,) * 6,
        scratch_shapes=list(SCRATCH.values()),
        compiler_params=pltpu.CompilerParams(
            collective_id=0, has_side_effects=True, vmem_limit_bytes=60 << 20
        ),
        name="repa_step",
    )(
        queries[0], key_states[0], value_states[0], residual[0], enc_hidden[0],
        enc_gain, enc_bias, feature_target, timestep, gate_weight, lift_weight, out_weight,
    )
    d_queries, d_keys, d_values, grad_gate, grad_lift, grad_out = pl.pallas_call(
        copy_kernel,
        out_shape=out_shape,
        grid=(2,),
        in_specs=[pl.BlockSpec((a.shape[0] // 2, a.shape[1]), lambda i: (i, 0)) for a in out_shape],
        out_specs=[pl.BlockSpec((a.shape[0] // 2, a.shape[1]), lambda i: (i, 0)) for a in out_shape],
        compiler_params=pltpu.CompilerParams(vmem_limit_bytes=60 << 20),
        name="hand_out",
    )(*outs)
    return (d_queries[None], d_keys[None], d_values[None], grad_gate, grad_lift, grad_out)


def solution(mesh):
    tokens = P("dp", "seq", None)
    rows = P("dp", None)
    in_specs = (tokens,) * 5 + (P(), P(), P("dp", "seq"), P("dp"), rows, rows, rows)
    out_specs = (tokens,) * 3 + (rows,) * 3
    return jax.shard_map(
        shards, mesh=mesh, in_specs=in_specs, out_specs=out_specs, check_vma=False
    )
```
